32 devices in a mesh: group: 4 (over z), sub: 8 (over y, x, core).
Axes of the slice: x: 2, y: 2, z: 4, core: 2. Of those that a mesh axis runs over, the one named last changes fastest.
Arguments:
- modal_dofs: float32 [9, 35, 4096], P(None, None, ('group', 'sub')), may hold values from -6 to 6
- jacobians: float32 [3, 9, 9, 4096], P(None, None, None, ('group', 'sub')), may hold values from -1.25 to 1.25
- stiffness: float32 [3, 35, 35], replicated, may hold values from -1 to 1
- face_trace: float32 [4, 15, 35], replicated, may hold values from -1 to 1
- neighbour_trace: float32 [12, 15, 35], replicated, may hold values from -1 to 1
- own_flux: float32 [4, 9, 9, 4096], P(None, None, None, ('group', 'sub')), may hold values from -2 to 2
- neighbour_flux: float32 [4, 9, 9, 4096], P(None, None, None, ('group', 'sub')), may hold values from -2 to 2
- face_lift: float32 [4, 35, 15], replicated, may hold values from -0.75 to 0.75
- neighbour_code: int32 [4, 4096], P(None, ('group', 'sub')), may hold values from 0 to 1663, as said below
- rim_select: int32 [4096], P(('group', 'sub')), may hold values from 0 to 1535
- fault_element: int32 [2, 1024], P(None, ('group', 'sub')), may hold values from 0 to 127
- fault_face: int32 [2, 1024], P(None, ('group', 'sub')), may hold values from 0 to 3
- send_count: int32 [4, 32], P(None, ('group', 'sub')), may hold values from 0 to 8
- fault_trace: float32 [4, 49, 35], replicated, may hold values from -1 to 1
- fault_lift: float32 [4, 35, 49], replicated, may hold values from -0.875 to 0.875
- coupling: float32 [9, 2], replicated, may hold values from -4 to 4
- fault_state: float32 [49, 1024], P(None, ('group', 'sub')), may hold values from -1 to 1
- direct_effect: float32 [49, 1024], P(None, ('group', 'sub')), may hold values from 0.5 to 1.5
- evolution_rate: float32 [49, 1024], P(None, ('group', 'sub')), may hold values from 0.5 to 2
Outputs:
- new_dofs: float32 [9, 35, 4096], P(None, None, ('group', 'sub'))
- new_state: float32 [49, 1024], P(None, ('group', 'sub'))
The draws below stay inside these ranges and needn't reach their ends.
Inputs may be any that keep to these rules, and one draw needn't show every extreme that they name: `neighbour_code`: face 0 of local elements 0 to 127 reads neighbour-list row 1536 plus its local index; other entries are any row below 1536.
All inputs are finite; a program needn't handle non-finite values.
Results may differ from the reference program's by a relative error of at most 0.0003.
Values sent between devices are 32-bit elements; how exact they have to be, the bound alone decides.
A program may use at most 128 MiB of HBM per device.

```python
import math
import jax
import jax.numpy as jnp
from jax import lax

NF = 9
NB = 35
NFM = 15
NQ = 49
DERIV = 4
NEWTON = 3
E_DEV = 128
FB = 64
CAP = 8
NE = 4096
SLOT_DEV = 32
SLOTS = 1024
N_GROUP = 4
N_SUB = 8
DEVICES = 32


def draw_neighbour_code(key, part):
    codes = jax.random.randint(key, (4, NE), 0, 12 * E_DEV).astype(jnp.int32)
    local = jnp.arange(NE, dtype=jnp.int32) % E_DEV
    rim_code = 12 * E_DEV + local
    first = jnp.where(local < 2 * FB, rim_code, codes[0])
    return codes.at[0].set(first)


def draw_send_count(key, part):
    counts = jax.random.randint(key, (SLOT_DEV // CAP, NE // E_DEV), 0, CAP + 1).astype(jnp.int32)
    return counts.at[0, 0].set(CAP)


def touch_ends(drawn, own_key, low, high):
    spot = [jax.random.randint(jax.random.fold_in(own_key, axis), (), 0, length) for axis, length in enumerate(drawn.shape)]
    widest = drawn.shape.index(max(drawn.shape))
    neighbour = spot[:widest] + [(spot[widest] + 1) % drawn.shape[widest]] + spot[widest + 1:]
    return drawn.at[tuple(spot)].set(low).at[tuple(neighbour)].set(high)


def steps_of(own_key, dims, cuts, low, high):
    def one(dim, parts):
        steps = jax.random.uniform(jax.random.fold_in(jax.random.fold_in(own_key, 6), dim), (parts,), jnp.float32, low / len(cuts), high / len(cuts))
        return jnp.repeat(jnp.exp(steps), dims[dim] // parts).reshape((-1,) + (1,) * (len(dims) - dim - 1))

    factor_of = one(*cuts[0])
    for cut in cuts[1:]:
        factor_of = factor_of * one(*cut)
    return factor_of


def scatter_about(stream_key, extent, deviation, reach, cuts=(), kind=jnp.bfloat16):
    gain = steps_of(stream_key, extent, cuts, -0.22, 0.18) if cuts else 1.0
    entries = jax.random.normal(stream_key, extent, jnp.float32) * deviation * gain
    return jnp.minimum(jnp.maximum(entries, -reach), reach).astype(kind)


def setup_inputs(seed: int = 0) -> dict:
    key_of = jax.random.split(jax.random.key(seed), 20)
    return {
        "modal_dofs": scatter_about(key_of[0], (NF, NB, NE), 1.0, 6.0, ((2, 32),), jnp.float32),
        "jacobians": scatter_about(key_of[1], (3, NF, NF, NE), (3 * NF) ** -0.5, 1.25, ((3, 32),), jnp.float32),
        "stiffness": scatter_about(key_of[2], (3, NB, NB), NB ** -0.5, 1.0, (), jnp.float32),
        "face_trace": scatter_about(key_of[3], (4, NFM, NB), NB ** -0.5, 1.0, (), jnp.float32),
        "neighbour_trace": scatter_about(key_of[4], (12, NFM, NB), NB ** -0.5, 1.0, (), jnp.float32),
        "own_flux": scatter_about(key_of[5], (4, NF, NF, NE), NF ** -0.5, 2.0, ((3, 32),), jnp.float32),
        "neighbour_flux": scatter_about(key_of[6], (4, NF, NF, NE), NF ** -0.5, 2.0, ((3, 32),), jnp.float32),
        "face_lift": scatter_about(key_of[7], (4, NB, NFM), (4 * NFM) ** -0.5, 0.75, (), jnp.float32),
        "neighbour_code": draw_neighbour_code(jax.random.fold_in(key_of[19], 71), 0),
        "rim_select": touch_ends(jax.random.randint(key_of[9], (2 * FB * DEVICES,), 0, 12 * E_DEV), jax.random.fold_in(key_of[9], 1), 0, (12 * E_DEV) - 1).astype(jnp.int32),
        "fault_element": touch_ends(jax.random.randint(key_of[10], (2, SLOTS), 0, E_DEV), jax.random.fold_in(key_of[10], 1), 0, E_DEV - 1).astype(jnp.int32),
        "fault_face": touch_ends(jax.random.randint(key_of[11], (2, SLOTS), 0, 4), jax.random.fold_in(key_of[11], 1), 0, 3).astype(jnp.int32),
        "send_count": draw_send_count(jax.random.fold_in(key_of[19], 71), 0),
        "fault_trace": scatter_about(key_of[13], (4, NQ, NB), NB ** -0.5, 1.0, (), jnp.float32),
        "fault_lift": scatter_about(key_of[14], (4, NB, NQ), NQ ** -0.5, 0.875, (), jnp.float32),
        "coupling": scatter_about(key_of[15], (NF, 2), 1.0, 4.0, (), jnp.float32),
        "fault_state": jnp.clip(jax.random.uniform(key_of[16], (NQ, SLOTS), jnp.float32, -1.0, 1.0) * steps_of(key_of[16], (NQ, SLOTS), ((1, 32),), -0.4, 0.0), -1.0, 1.0),
        "direct_effect": jnp.clip(0.5 + 1.0 * jax.random.uniform(key_of[17], (NQ, SLOTS), jnp.float32) ** steps_of(key_of[17], (NQ, SLOTS), ((1, 32),), -0.2, 0.2), 0.5, 1.5),
        "evolution_rate": jnp.clip(jnp.exp(math.log(2.0) - 1.3862944 * jax.random.uniform(key_of[18], (NQ, SLOTS), jnp.float32) ** steps_of(key_of[18], (NQ, SLOTS), ((1, 32),), -0.2, 0.2)), 0.5, 2.0),
    }


PRECISE = lax.Precision.HIGHEST
IMPEDANCE = 1.0
NORMAL_LOAD = 2.0

def inverse_sinh(value):
    return jnp.sign(value) * jnp.log(jnp.abs(value) + jnp.sqrt(1.0 + value * value))

def predict(modal_dofs, jacobians, stiffness):
    derivative = modal_dofs
    integral = modal_dofs
    factorial = 1.0
    for degree in range(1, DERIV + 1):
        mixed_terms = jnp.einsum('dfge,gce->dfce', jacobians, derivative, precision=PRECISE)
        derivative = -jnp.einsum('dbc,dfce->fbe', stiffness, mixed_terms, precision=PRECISE)
        factorial = factorial * (degree + 1)
        integral = integral + derivative / factorial
    mixed_terms = jnp.einsum('dfge,gce->dfce', jacobians, integral, precision=PRECISE)
    volume = jnp.einsum('dcb,dfce->fbe', stiffness, mixed_terms, precision=PRECISE)
    return (integral, volume)

def trace_table(integral, neighbour_trace):
    table = jnp.einsum('kqc,fce->fqke', neighbour_trace, integral, precision=PRECISE)
    return table.reshape(table.shape[0], table.shape[1], -1)

def side_traces(integral, fault_element, fault_face, fault_trace):
    side_values = jnp.take(integral, fault_element, axis=2)
    point_maps = jnp.take(fault_trace, fault_face, axis=0)
    traces = jnp.einsum('ispc,fcis->ifps', point_maps, side_values, precision=PRECISE)
    return traces.reshape((-1,) + traces.shape[2:])

def pick_fields(sides):
    half = sides.shape[0] // 2
    return jnp.stack([sides[0], sides[3], sides[7], sides[half], sides[half + 3], sides[half + 7]])

def friction(picked, fault_state, direct_effect, evolution_rate):
    normal_mean = 0.5 * (picked[0] + picked[3])
    locked = 0.5 * (picked[1] + picked[4]) + 0.5 * IMPEDANCE * (picked[5] - picked[2])
    normal_load = jnp.logaddexp(0.0, NORMAL_LOAD - normal_mean)
    magnitude = jnp.abs(locked)
    rate_scale = 0.5 * jnp.exp(fault_state / direct_effect)
    strength = normal_load * direct_effect
    slip = jnp.zeros_like(magnitude)
    for sweep in range(NEWTON):
        scaled = rate_scale * slip
        mismatch = IMPEDANCE * slip + strength * inverse_sinh(scaled) - magnitude
        slope = IMPEDANCE + strength * rate_scale / jnp.sqrt(1.0 + scaled * scaled)
        slip = slip - mismatch / slope
    signed_slip = jnp.sign(locked) * slip
    traction = locked - IMPEDANCE * signed_slip
    new_state = fault_state + 0.5 * evolution_rate * (jnp.exp(-fault_state) - slip)
    return (jnp.stack([traction, signed_slip]), new_state)

def fault_correction(traces, answer, fault_element, fault_face, fault_lift, coupling, live_slots, elements):
    half = traces.shape[0] // 2
    minus = traces[:half]
    plus = traces[half:]
    traction = answer[0]
    signed_slip = answer[1]
    jump_minus = 0.5 * (plus[7] - minus[7]) - 0.5 * signed_slip
    jump_plus = 0.5 * (minus[7] - plus[7]) + 0.5 * signed_slip
    drive_minus = coupling[:, 0, None, None] * (traction - minus[3]) + coupling[:, 1, None, None] * jump_minus
    drive_plus = coupling[:, 0, None, None] * (traction - plus[3]) + coupling[:, 1, None, None] * jump_plus
    drive = jnp.stack([drive_minus, drive_plus])
    lift_maps = jnp.take(fault_lift, fault_face, axis=0)
    lifted = jnp.einsum('isbp,ifps->ifbs', lift_maps, drive, precision=PRECISE)
    matches = fault_element[:, :, None] == jnp.arange(elements, dtype=jnp.int32)[None, None, :]
    scatter_mask = (matches & live_slots[None, :, None]).astype(jnp.float32)
    return jnp.einsum('ifbs,ise->fbe', lifted, scatter_mask, precision=PRECISE)

def surface_update(modal_dofs, integral, volume, face_trace, own_flux, neighbour_flux, face_lift, neighbour_code, extended):
    own_traces = jnp.einsum('jqc,fce->jfqe', face_trace, integral, precision=PRECISE)
    neighbour_traces = jnp.take(extended, neighbour_code, axis=2)
    face_flux = jnp.einsum('jfge,jgqe->jfqe', own_flux, own_traces, precision=PRECISE)
    face_flux = face_flux + jnp.einsum('jfge,gqje->jfqe', neighbour_flux, neighbour_traces, precision=PRECISE)
    surface = jnp.einsum('jbq,jfqe->fbe', face_lift, face_flux, precision=PRECISE)
    return modal_dofs + volume - surface

def reference(modal_dofs, jacobians, stiffness, face_trace, neighbour_trace, own_flux, neighbour_flux, face_lift, neighbour_code, rim_select, fault_element, fault_face, send_count, fault_trace, fault_lift, coupling, fault_state, direct_effect, evolution_rate):
    devices = N_GROUP * N_SUB

    def to_devices(whole):
        split = whole.reshape(whole.shape[:-1] + (devices, whole.shape[-1] // devices))
        return jnp.moveaxis(split, -2, 0)

    def from_devices(pieces):
        moved = jnp.moveaxis(pieces, 0, -2)
        return moved.reshape(moved.shape[:-2] + (-1,))
    dofs_dev = to_devices(modal_dofs)
    jacobians_dev = to_devices(jacobians)
    rims_dev = to_devices(rim_select)
    elements_dev = to_devices(fault_element)
    faces_dev = to_devices(fault_face)

    def first_phase(pieces):
        dofs_here, jacobians_here, rims_here, elements_here, faces_here = pieces
        integral, volume = predict(dofs_here, jacobians_here, stiffness)
        table = trace_table(integral, neighbour_trace)
        rim_rows = jnp.take(table, rims_here, axis=2)
        traces = side_traces(integral, elements_here, faces_here, fault_trace)
        return (integral, volume, rim_rows, traces)
    integral, volume, rim_rows, traces = lax.map(first_phase, (dofs_dev, jacobians_dev, rims_dev, elements_dev, faces_dev))
    grid = rim_rows.reshape((N_GROUP, N_SUB) + rim_rows.shape[1:])
    empty = jnp.zeros_like(grid[:, :1])
    from_before = jnp.concatenate([empty, grid[:, :-1]], axis=1)[..., FB:]
    from_after = jnp.concatenate([grid[:, 1:], empty], axis=1)[..., :FB]
    from_before = from_before.reshape((devices,) + from_before.shape[2:])
    from_after = from_after.reshape((devices,) + from_after.shape[2:])
    slots = traces.shape[-1]
    trace_grid = traces.reshape((N_GROUP, N_SUB) + traces.shape[1:3] + (N_GROUP, CAP))
    received = jnp.swapaxes(trace_grid, 0, 4).reshape(traces.shape)
    received = jnp.moveaxis(received, 1, 0)
    answer, new_state = friction(pick_fields(received), to_devices(fault_state), to_devices(direct_effect), to_devices(evolution_rate))
    answer = jnp.moveaxis(answer, 0, 1)
    answer_grid = answer.reshape((N_GROUP, N_SUB) + answer.shape[1:3] + (N_GROUP, CAP))
    answer = jnp.swapaxes(answer_grid, 0, 4).reshape(answer.shape)
    counts_dev = to_devices(send_count)[:, :, 0]
    live_dev = (jnp.arange(slots, dtype=jnp.int32) % CAP)[None, :] < jnp.repeat(counts_dev, CAP, axis=1)
    codes_dev = to_devices(neighbour_code)
    own_dev = to_devices(own_flux)
    far_dev = to_devices(neighbour_flux)

    def second_phase(pieces):
        dofs_here, integral_here, volume_here, codes_here, own_here, far_here, before_here, after_here, traces_here, answer_here, elements_here, faces_here, live_here = pieces
        table = trace_table(integral_here, neighbour_trace)
        extended = jnp.concatenate([table, before_here, after_here], axis=2)
        updated = surface_update(dofs_here, integral_here, volume_here, face_trace, own_here, far_here, face_lift, codes_here, extended)
        return updated + fault_correction(traces_here, answer_here, elements_here, faces_here, fault_lift, coupling, live_here, dofs_here.shape[2])
    new_dofs = lax.map(second_phase, (dofs_dev, integral, volume, codes_dev, own_dev, far_dev, from_before, from_after, traces, answer, elements_dev, faces_dev, live_dev))
    return (from_devices(new_dofs), from_devices(new_state))
```

```python
import functools

import jax
import jax.numpy as jnp
from jax import lax
from jax.experimental import pallas as pl
from jax.experimental.pallas import tpu as pltpu
from jax.sharding import PartitionSpec as P

DERIV = 4
NEWTON = 3
CAP = 8
F32 = jnp.float32
BF16 = jnp.bfloat16
MESH = pl.DeviceIdType.MESH


def up(n, m):
    return (n + m - 1) // m * m


def halves(x):
    high = x.astype(BF16).astype(F32)
    return high, x - high


def stacked(parts, rows):
    have = sum(p.shape[0] for p in parts)
    if have < rows:
        parts = parts + [jnp.zeros((rows - have, parts[0].shape[1]), F32)]
    return jnp.concatenate(parts, axis=0).astype(BF16)


def mul(a, b):
    return lax.dot_general(a, b, (((1,), (0,)), ((), ())), preferred_element_type=F32)


def roll(x, shift):
    return pltpu.roll(x, shift, 1)


def lanes3(a, step):
    high, low = halves(a)
    return (high + roll(low, step) + roll(high, 2 * step)).astype(BF16)


def friction(normal, locked, state, direct):
    rate = 0.5 * jnp.exp(state / direct)
    x = 2.0 - normal
    load = jnp.maximum(x, 0.0) + jnp.log1p(jnp.exp(-jnp.abs(x)))
    strength = load * direct
    magnitude = jnp.abs(locked)
    slip = magnitude / (1.0 + strength * rate)
    for _ in range(1, NEWTON):
        scaled = rate * slip
        root = jnp.sqrt(1.0 + scaled * scaled)
        log = jnp.log(jnp.abs(scaled) + root)
        log = jnp.where(scaled < 0.0, -log, log)
        slip = slip - (slip + strength * log - magnitude) / (1.0 + strength * rate / root)
    return slip


N_IN = 19
ORDER = (2, 0, 1, 10, 13, 16, 17, 4, 3, 9, 8, 7, 11, 14, 18, 12, 15, 5, 6)


def kernel(n_group, n_sub, *refs):
    hbm, out, out_state = refs[:N_IN], refs[N_IN], refs[N_IN + 1]
    local = refs[N_IN + 2 : 2 * N_IN]
    (
        par,
        integ,
        parts,
        table,
        own,
        near,
        flux,
        base,
        w_stiff,
        w_face,
        w_near,
        w_ftrace,
        w_flift,
        w_lift,
        rim_send,
        rim_recv,
        fric_send,
        fric_recv,
        par_recv,
        slip_pad,
        stage_sem,
        send_sem,
        recv_sem,
    ) = refs[2 * N_IN :]
    me_g = lax.axis_index("group")
    me_s = lax.axis_index("sub")
    prev_s = lax.rem(me_s + n_sub - 1, n_sub)
    next_s = lax.rem(me_s + 1, n_sub)
    barrier = pltpu.get_barrier_semaphore()
    for d in range(1, n_group):
        pl.semaphore_signal(
            barrier, inc=1, device_id=(lax.rem(me_g + d, n_group), me_s), device_id_type=MESH
        )
    for s in (prev_s, next_s):
        pl.semaphore_signal(barrier, inc=1, device_id=(me_g, s), device_id_type=MESH)

    held = list(local[:16]) + [par.at[0], par.at[1]] + list(local[16:])
    staged = {i: pltpu.make_async_copy(hbm[i], held[i], stage_sem.at[i]) for i in ORDER}
    for i in ORDER:
        staged[i].start()

    def arrive(*which):
        for i in which:
            staged[i].wait()

    (
        dofs,
        jac,
        stiff,
        face_trace,
        neighbour_trace,
        own_flux,
        neighbour_flux,
        face_lift,
        code,
        rim,
        fault_element,
        fault_face,
        send_count,
        fault_trace,
        fault_lift,
        coupling,
    ) = held[:16]
    evolution_rate = held[18]
    nf, nb, elems = dofs.shape
    ndim = stiff.shape[0]
    nfm, nj, _ = face_trace.shape
    nk = neighbour_trace.shape[0]
    _, nface, nq = fault_trace.shape
    slots = fault_element.shape[1]
    cp, fp, qp = up(nb, 8), up(nfm, 8), up(nq, 8)
    width = 4 * slots

    w_stiff[...] = jnp.zeros_like(w_stiff)
    w_ftrace[...] = jnp.zeros_like(w_ftrace)
    w_face[...] = jnp.zeros_like(w_face)
    w_near[...] = jnp.zeros_like(w_near)
    w_flift[...] = jnp.zeros_like(w_flift)
    w_lift[...] = jnp.zeros_like(w_lift)
    slip_pad[...] = jnp.zeros_like(slip_pad)

    arrive(2)
    for d in range(ndim):
        w_stiff[d * cp : d * cp + nb, :nb] = stiff[d]
    a_stiff = lanes3(-w_stiff[...], cp)
    many = 3 if nf % 3 == 0 else 1
    rows = ndim * cp

    def spread_out(fields):
        out = []
        for x in fields:
            high, low = halves(x)
            out.append(stacked([high, high, low], 128))
        return jnp.concatenate(out, axis=1)

    def mixed(turn, f):
        sums = [None] * many
        for g in range(nf):
            for d in range(ndim):
                x = parts[turn, g, d * cp : (d + 1) * cp]
                for m in range(many):
                    term = jac[f + m, g, pl.ds(d, 1), :] * x
                    sums[m] = term if sums[m] is None else sums[m] + term
        return sums

    arrive(0)
    for f in range(0, nf, many):
        group = [
            jnp.concatenate([dofs[f + m], jnp.zeros((cp - nb, elems), F32)], axis=0)
            for m in range(many)
        ]
        r = mul(a_stiff, spread_out(group))
        for m in range(many):
            integ[f + m] = group[m]
            parts[0, f + m] = r[:, m * elems : (m + 1) * elems]

    arrive(1)
    factorial = 1.0
    for degree in range(1, DERIV + 1):
        factorial = factorial * (degree + 1)
        turn = (degree - 1) % 2
        for f in range(0, nf, many):
            group = mixed(turn, f)
            for m in range(many):
                integ[f + m] = integ[f + m] + group[m] / factorial
            if degree < DERIV:
                r = mul(a_stiff, spread_out(group))
                for m in range(many):
                    parts[1 - turn, f + m] = r[:, m * elems : (m + 1) * elems]

    arrive(10, 11, 13)
    for k in range(nface):
        for b in range(nb):
            w_ftrace[k, b : b + 1, :nq] = fault_trace[b, pl.ds(k, 1), :]
    lane = lax.broadcasted_iota(jnp.int32, (1, width), 1)
    is_v1 = (lane & slots) != 0
    sign_i = jnp.where((lane & (2 * slots)) != 0, 1.0, -1.0).astype(F32)
    slot_group = (lane & (slots - 1)) // CAP
    elem = fault_element[...]
    face = fault_face[...]
    elem_row = jnp.concatenate([elem[0:1], elem[0:1], elem[1:2], elem[1:2]], axis=1)
    face_row = jnp.concatenate([face[0:1], face[0:1], face[1:2], face[1:2]], axis=1)
    hit = lax.broadcasted_iota(jnp.int32, (elems, width), 0) == elem_row
    hot = jnp.where(hit, 1.0, 0.0).astype(F32)

    i0, i3, i7 = integ[0], integ[3], integ[7]
    highs, lows = zip(*[halves(x) for x in (i0, i3, i7)])
    g = mul(stacked(list(highs) + list(lows), 6 * cp), hot.astype(BF16))
    g = g[: 3 * cp] + g[3 * cp :]
    g0, g3, g7 = g[:cp], g[cp : 2 * cp], g[2 * cp :]
    a_fault = []
    for k in range(nface):
        high, low = halves(w_ftrace[k])
        gap = jnp.zeros((128 - 3 * cp, 128), F32)
        a_fault.append(jnp.concatenate([high, low, high, gap], axis=0).T[:qp])
    a_fault = jnp.concatenate(a_fault, axis=0).astype(BF16)

    def fault_sides(x):
        high, low = halves(x)
        y = mul(a_fault, stacked([high, high, low], 128))
        total = jnp.where(face_row == 0, y[:qp], 0.0)
        for k in range(1, nface):
            total = jnp.where(face_row == k, y[k * qp : (k + 1) * qp], total)
        return total

    mean = fault_sides(jnp.where(is_v1, 0.5 * g3 + (0.5 * sign_i) * g7, 0.5 * g0))
    mean = mean + roll(mean, 2 * slots)
    mean_t = jnp.concatenate([mean, jnp.zeros((128 - qp, width), F32)], axis=0).T
    normal_here = mean_t[:slots, :nq]
    locked_here = mean_t[slots : 2 * slots, :nq]
    fric_send[0] = normal_here
    fric_send[1] = locked_here
    sides = fault_sides(jnp.where(is_v1, g7, g3))
    arrive(16, 17)

    pl.semaphore_wait(barrier, n_group + 1)

    here = pl.ds(pl.multiple_of(me_g * CAP, CAP), CAP)
    par_copies, fric_copies = [], []
    for src, dst, first, copies in (
        (par, par_recv, 0, par_copies),
        (fric_send, fric_recv, n_group - 1, fric_copies),
    ):
        for d in range(1, n_group):
            o = lax.rem(me_g + d, n_group)
            there = pl.ds(pl.multiple_of(o * CAP, CAP), CAP)
            copy = pltpu.make_async_remote_copy(
                src_ref=src.at[:, there, :],
                dst_ref=dst.at[:, here, :],
                send_sem=send_sem.at[first + d - 1],
                recv_sem=recv_sem.at[first + d - 1],
                device_id=(o, me_s),
                device_id_type=MESH,
            )
            copy.start()
            copies.append(copy)
        dst[:, here, :] = src[:, here, :]

    arrive(3, 4)
    for k in range(nk):
        w_near[k * fp : k * fp + nfm, :nb] = neighbour_trace[k]
    for j in range(nj):
        for q in range(nfm):
            w_face[j * fp + q : j * fp + q + 1, :nb] = face_trace[q, pl.ds(j, 1), :]
    gap = jnp.zeros((128 - cp, 128), F32)
    v = [jnp.concatenate([w_stiff[d * cp : (d + 1) * cp], gap], axis=0).T[:cp] for d in range(ndim)]
    a_last = jnp.concatenate(
        [lanes3(jnp.concatenate(v, axis=0), cp), lanes3(w_near[...], cp), lanes3(w_face[...], cp)],
        axis=0,
    )
    turn = DERIV % 2
    for f in range(0, nf, many):
        r = mul(a_last, spread_out([integ[f + m] for m in range(many)]))
        for m in range(many):
            y = r[:, m * elems : (m + 1) * elems]
            parts[turn, f + m] = y[:rows]
            table[f + m] = y[rows : rows + nk * fp]
            y = y[rows + nk * fp :]
            for j in range(nj):
                own[j, f + m] = y[j * fp : (j + 1) * fp]

    arrive(8, 9)
    def near_traces(rows, store):
        groups, picks = [], []
        for row in rows:
            group = jnp.zeros_like(row)
            for k in range(1, nk):
                group = group + jnp.where(row >= k * elems, 1, 0)
            groups.append(jnp.broadcast_to(group, (fp, elems)))
            picks.append(jnp.broadcast_to(row - group * elems, (fp, elems)))

        def step(f, carry):
            totals = [jnp.zeros((fp, elems), F32) for _ in rows]
            for k in range(nk):
                x = table[f, k * fp : (k + 1) * fp]
                for i, pick in enumerate(picks):
                    got = jnp.take_along_axis(x, pick, axis=1, mode="promise_in_bounds")
                    totals[i] = jnp.where(groups[i] == k, got, totals[i])
            store(f, totals)
            return carry

        lax.fori_loop(0, nf, step, 0, unroll=many)

    def store_rim(f, totals):
        rim_send[f] = totals[0]

    near_traces([roll(rim[...], elems // 2)], store_rim)

    def store_near(f, totals):
        for j in range(1, nj):
            near[j - 1, f] = totals[j - 1]

    first = 2 * (n_group - 1)
    rim_copies = []
    for side, s in enumerate((next_s, prev_s)):
        copy = pltpu.make_async_remote_copy(
            src_ref=rim_send,
            dst_ref=rim_recv.at[side],
            send_sem=send_sem.at[first + side],
            recv_sem=recv_sem.at[first + side],
            device_id=(me_g, s),
            device_id_type=MESH,
        )
        copy.start()
        rim_copies.append(copy)

    near_traces([code[j : j + 1, :] for j in range(1, nj)], store_near)

    for f in range(0, nf, many):
        group = mixed(turn, f)
        for m in range(many):
            base[f + m] = group[m]

    arrive(5, 6, 7)
    for j in range(nj):
        for q in range(nfm):
            w_lift[j * fp + q : j * fp + q + 1, :nb] = face_lift[q, pl.ds(j, 1), :]
    def face_flux(j, at_row, field):
        def step(i, carry):
            f = i * many
            sums = [None] * many
            for g in range(nf):
                mine, other = own[j, g], field(g)
                for m in range(many):
                    term = own_flux[f + m, g, pl.ds(j, 1), :] * mine
                    term = term + neighbour_flux[f + m, g, pl.ds(j, 1), :] * other
                    sums[m] = term if sums[m] is None else sums[m] + term
            for m in range(many):
                at = pl.ds(pl.multiple_of((f + m) * elems, elems), elems)
                flux[at_row : at_row + fp, at] = sums[m]
            return carry

        lax.fori_loop(0, nf // many, step, 0)

    kj = (nj - 1) * fp
    kr = up(kj, 16)
    for j in range(1, nj):
        face_flux(j, (j - 1) * fp, lambda g, j=j: near[j - 1, g])
    lift_all = w_lift[...].T[:cp]
    lift = roll(lift_all, 128 - fp)
    l_hi, l_lo = halves(lift)
    l_hi, l_lo = l_hi[:, :kr], l_lo[:, :kr]
    k_lane = lax.broadcasted_iota(jnp.int32, lift_all.shape, 1)
    x = flux[:kj]
    high, low = halves(x)
    x_hi = stacked([high], kr)
    r = mul(stacked([l_hi, l_lo], 2 * cp), x_hi)
    r = r[:cp] + r[cp:] + mul(l_hi.astype(BF16), stacked([low], kr))
    for f in range(nf):
        base[f] = base[f] - r[:, f * elems : (f + 1) * elems]

    for copy in par_copies:
        copy.wait_recv()
    slip = friction(normal_here, locked_here, par_recv[0], par_recv[1])
    signed = jnp.where(locked_here < 0.0, -slip, jnp.where(locked_here > 0.0, slip, 0.0))
    for i in range(4):
        slip_pad[i * slots : (i + 1) * slots, :nq] = signed

    arrive(12, 14, 15)
    for k in range(nface):
        for b in range(nb):
            w_flift[k * cp + b : k * cp + b + 1, :nq] = fault_lift[b, pl.ds(k, 1), :]
    live = jnp.zeros_like(lane)
    for o in range(n_group):
        live = jnp.where(slot_group == o, send_count[0, o], live)
    live = (lane & (CAP - 1)) < live
    side = jnp.where(live, face_row, -1)
    hot0 = jnp.where(is_v1, 0.0, hot)
    hot1 = jnp.where(is_v1, hot, 0.0)
    spread = stacked([hot0, hot1], 2 * elems)
    f_hi, f_lo = halves(w_flift[...])
    kq = 64
    a_lift = jnp.concatenate([f_hi + roll(f_lo, kq), f_hi], axis=1)[:, : 3 * kq].astype(BF16)
    turned = roll(mean, slots)
    locked = jnp.where(is_v1, mean, turned)
    drive_0 = jnp.where(is_v1, 0.5 * (roll(sides, 2 * slots) - sides), locked - sides)
    drive_1 = jnp.where(is_v1, 0.5 * sign_i, -1.0)
    answer = slip_pad[...].T[:qp]
    drive = drive_0 + drive_1 * answer
    high, low = halves(drive)
    gap = jnp.zeros((kq - qp, width), F32)
    y = mul(a_lift, stacked([high, gap, high, gap, low, gap], 3 * kq))
    lifted = jnp.where(side == 0, y[:cp], 0.0)
    for k in range(1, nface):
        lifted = jnp.where(side == k, y[k * cp : (k + 1) * cp], lifted)
    high, low = halves(lifted)
    z = lax.dot_general(
        stacked([high, low], 2 * cp),
        spread,
        (((1,), (1,)), ((), ())),
        preferred_element_type=F32,
    )
    z = z[:cp] + z[cp:]
    by_traction, by_jump = z[:, :elems], z[:, elems:]
    for copy in rim_copies:
        copy.wait_recv()
    e_lane = lax.broadcasted_iota(jnp.int32, (1, elems), 1)
    has_prev = jnp.where(me_s > 0, 1, 0)
    has_next = jnp.where(me_s < n_sub - 1, 1, 0)
    from_prev = (e_lane < elems // 2) & (has_prev == 1)
    from_next = (e_lane >= elems // 2) & (has_next == 1)
    for f in range(nf):
        near[0, f] = jnp.where(
            from_prev, rim_recv[0, f], jnp.where(from_next, rim_recv[1, f], 0.0)
        )
    face_flux(0, 0, lambda g: near[0, g])
    high, low = halves(flux[:fp])
    l0 = lanes3(jnp.where(k_lane < fp, lift_all, 0.0), fp)[:, : 3 * fp]
    r = mul(l0, stacked([high, high, low], 3 * fp))

    for f in range(nf):
        add = coupling[0, f] * by_traction + coupling[1, f] * by_jump
        total = base[f] - r[:, f * elems : (f + 1) * elems] + add
        out[f] = dofs[f] + total[:nb]


    arrive(18)
    for copy in fric_copies:
        copy.wait_recv()
    state = par[0]
    slip = friction(fric_recv[0], fric_recv[1], state, par[1])
    out_state[...] = state + 0.5 * evolution_rate[...] * (jnp.exp(-state) - slip)

    for copy in par_copies + fric_copies + rim_copies:
        copy.wait_send()


def finish(dofs, state, out, out_state, sem):
    copies = [
        pltpu.make_async_copy(dofs, out, sem.at[0]),
        pltpu.make_async_copy(state, out_state, sem.at[1]),
    ]
    for copy in copies:
        copy.start()
    for copy in copies:
        copy.wait()


def body(*args):
    args = list(args)
    n_group, n_sub = lax.axis_size("group"), lax.axis_size("sub")
    orders = {1: (1, 2, 0, 3), 3: (1, 0, 2), 5: (1, 2, 0, 3), 6: (1, 2, 0, 3), 7: (2, 0, 1)}
    orders |= {13: (2, 0, 1), 14: (1, 0, 2)}
    orders |= {i: (1, 0) for i in (12, 15, 16, 17, 18)}
    for i, order in orders.items():
        args[i] = jnp.transpose(args[i], order)
    nf, nb, elems = args[0].shape
    nfm, nj, _ = args[3].shape
    nk = args[4].shape[0]
    ndim = args[2].shape[0]
    _, nface, nq = args[13].shape
    slots = args[10].shape[1]
    args[9] = args[9].reshape(1, elems)
    cp, fp, qp = up(nb, 8), up(nfm, 8), up(nq, 8)
    width = 4 * slots
    vmem = pl.BlockSpec(memory_space=pltpu.VMEM)
    anywhere = pl.BlockSpec(memory_space=pl.ANY)
    held = [(pltpu.SMEM if i in (12, 15) else pltpu.VMEM)(a.shape, a.dtype) for i, a in enumerate(args)]
    shapes = (args[0].shape, args[16].shape)
    copies = 2 * (n_group - 1) + 2
    dofs, state = pl.pallas_call(
        functools.partial(kernel, n_group, n_sub),
        out_shape=tuple(pltpu.VMEM(s, F32) for s in shapes),
        in_specs=[anywhere] * len(args),
        out_specs=(vmem, vmem),
        scratch_shapes=held[:16]
        + held[18:]
        + [
            pltpu.VMEM((2,) + args[16].shape, F32),
            pltpu.VMEM((nf, cp, elems), F32),
            pltpu.VMEM((2, nf, ndim * cp, elems), F32),
            pltpu.VMEM((nf, nk * fp, elems), F32),
            pltpu.VMEM((nj, nf, fp, elems), F32),
            pltpu.VMEM((nj, nf, fp, elems), F32),
            pltpu.VMEM((up((nj - 1) * fp, 16), nf * elems), F32),
            pltpu.VMEM((nf, cp, elems), F32),
            pltpu.VMEM((ndim * cp, 128), F32),
            pltpu.VMEM((nj * fp, 128), F32),
            pltpu.VMEM((nk * fp, 128), F32),
            pltpu.VMEM((nface, cp, 128), F32),
            pltpu.VMEM((nface * cp, 128), F32),
            pltpu.VMEM((128, 128), F32),
            pltpu.VMEM((nf, fp, elems), F32),
            pltpu.VMEM((2, nf, fp, elems), F32),
            pltpu.VMEM((2, slots, nq), F32),
            pltpu.VMEM((2, slots, nq), F32),
            pltpu.VMEM((2, slots, nq), F32),
            pltpu.VMEM((width, 128), F32),
            pltpu.SemaphoreType.DMA((len(args),)),
            pltpu.SemaphoreType.DMA((copies,)),
            pltpu.SemaphoreType.DMA((copies,)),
        ],
        compiler_params=pltpu.CompilerParams(collective_id=0, has_side_effects=True),
    )(*args)
    dofs, state = pl.pallas_call(
        finish,
        out_shape=tuple(jax.ShapeDtypeStruct(s, F32) for s in shapes),
        in_specs=[vmem, vmem],
        out_specs=(anywhere, anywhere),
        scratch_shapes=[pltpu.SemaphoreType.DMA((2,))],
        compiler_params=pltpu.CompilerParams(vmem_limit_bytes=8 << 20),
    )(dofs, state)
    return dofs, state.T


def solution(mesh):
    both = ("group", "sub")
    placed = (
        P(None, None, both),
        P(None, None, None, both),
        P(),
        P(),
        P(),
        P(None, None, None, both),
        P(None, None, None, both),
        P(),
        P(None, both),
        P(both),
        P(None, both),
        P(None, both),
        P(None, both),
        P(),
        P(),
        P(),
        P(None, both),
        P(None, both),
        P(None, both),
    )
    return jax.shard_map(
        body,
        mesh=mesh,
        in_specs=placed,
        out_specs=(P(None, None, both), P(None, both)),
        check_vma=False,
    )
```

```python
import functools

import jax
import jax.numpy as jnp
from jax import lax
from jax.experimental import pallas as pl
from jax.experimental.pallas import tpu as pltpu
from jax.sharding import PartitionSpec as P

DERIV = 4
NEWTON = 3
CAP = 8
F32 = jnp.float32
BF16 = jnp.bfloat16
MESH = pl.DeviceIdType.MESH


def up(n, m):
    return (n + m - 1) // m * m


def halves(x):
    high = x.astype(BF16).astype(F32)
    return high, x - high


def stacked(parts, rows):
    have = sum(p.shape[0] for p in parts)
    if have < rows:
        parts = parts + [jnp.zeros((rows - have, parts[0].shape[1]), F32)]
    return jnp.concatenate(parts, axis=0).astype(BF16)


def mul(a, b):
    return lax.dot_general(a, b, (((1,), (0,)), ((), ())), preferred_element_type=F32)


def roll(x, shift):
    return pltpu.roll(x, shift, 1)


def lanes3(a, step):
    high, low = halves(a)
    return (high + roll(low, step) + roll(high, 2 * step)).astype(BF16)


def friction(normal, locked, state, direct):
    rate = 0.5 * jnp.exp(state / direct)
    x = 2.0 - normal
    load = jnp.maximum(x, 0.0) + jnp.log1p(jnp.exp(-jnp.abs(x)))
    strength = load * direct
    magnitude = jnp.abs(locked)
    slip = magnitude / (1.0 + strength * rate)
    for _ in range(1, NEWTON):
        scaled = rate * slip
        root = jnp.sqrt(1.0 + scaled * scaled)
        log = jnp.log(jnp.abs(scaled) + root)
        log = jnp.where(scaled < 0.0, -log, log)
        slip = slip - (slip + strength * log - magnitude) / (1.0 + strength * rate / root)
    return slip


N_IN = 19
ORDER = (2, 0, 1, 10, 13, 16, 17, 4, 3, 9, 8, 7, 11, 14, 18, 12, 15, 5, 6)


def kernel(n_group, n_sub, *refs):
    hbm, out, out_state = refs[:N_IN], refs[N_IN], refs[N_IN + 1]
    local = refs[N_IN + 2 : 2 * N_IN]
    (
        par,
        integ,
        parts,
        gathered,
        own,
        near,
        flux,
        base,
        w_stiff,
        w_face,
        w_near,
        w_ftrace,
        w_flift,
        w_lift,
        rim_send,
        rim_recv,
        fric_send,
        fric_recv,
        par_recv,
        slip_pad,
        stage_sem,
        send_sem,
        recv_sem,
    ) = refs[2 * N_IN :]
    me_g = lax.axis_index("group")
    me_s = lax.axis_index("sub")
    prev_s = lax.rem(me_s + n_sub - 1, n_sub)
    next_s = lax.rem(me_s + 1, n_sub)
    barrier = pltpu.get_barrier_semaphore()
    for d in range(1, n_group):
        pl.semaphore_signal(
            barrier, inc=1, device_id=(lax.rem(me_g + d, n_group), me_s), device_id_type=MESH
        )
    for s in (prev_s, next_s):
        pl.semaphore_signal(barrier, inc=1, device_id=(me_g, s), device_id_type=MESH)

    held = list(local[:16]) + [par.at[0], par.at[1]] + list(local[16:])
    staged = {i: pltpu.make_async_copy(hbm[i], held[i], stage_sem.at[i]) for i in ORDER}
    for i in ORDER:
        staged[i].start()

    def arrive(*which):
        for i in which:
            staged[i].wait()

    (
        dofs,
        jac,
        stiff,
        face_trace,
        neighbour_trace,
        own_flux,
        neighbour_flux,
        face_lift,
        code,
        rim,
        fault_element,
        fault_face,
        send_count,
        fault_trace,
        fault_lift,
        coupling,
    ) = held[:16]
    evolution_rate = held[18]
    nf, nb, elems = dofs.shape
    ndim = stiff.shape[0]
    nfm, nj, _ = face_trace.shape
    nk = neighbour_trace.shape[0]
    _, nface, nq = fault_trace.shape
    slots = fault_element.shape[1]
    cp, fp, qp = up(nb, 8), up(nfm, 8), up(nq, 8)
    width = 4 * slots

    w_stiff[...] = jnp.zeros_like(w_stiff)
    w_ftrace[...] = jnp.zeros_like(w_ftrace)
    w_face[...] = jnp.zeros_like(w_face)
    w_near[...] = jnp.zeros_like(w_near)
    w_flift[...] = jnp.zeros_like(w_flift)
    w_lift[...] = jnp.zeros_like(w_lift)
    slip_pad[...] = jnp.zeros_like(slip_pad)

    here = pl.ds(pl.multiple_of(me_g * CAP, CAP), CAP)

    def to_group(src, dst, first):
        copies = []
        for d in range(1, n_group):
            o = lax.rem(me_g + d, n_group)
            there = pl.ds(pl.multiple_of(o * CAP, CAP), CAP)
            copies.append(
                pltpu.make_async_remote_copy(
                    src_ref=src.at[:, there, :],
                    dst_ref=dst.at[:, here, :],
                    send_sem=send_sem.at[first + d - 1],
                    recv_sem=recv_sem.at[first + d - 1],
                    device_id=(o, me_s),
                    device_id_type=MESH,
                )
            )
        return copies

    par_copies = to_group(par, par_recv, 0)
    fric_copies = to_group(fric_send, fric_recv, n_group - 1)
    rim_copies = []
    for side, s in enumerate((next_s, prev_s)):
        rim_copies.append(
            pltpu.make_async_remote_copy(
                src_ref=rim_send,
                dst_ref=rim_recv.at[side],
                send_sem=send_sem.at[2 * (n_group - 1) + side],
                recv_sem=recv_sem.at[2 * (n_group - 1) + side],
                device_id=(me_g, s),
                device_id_type=MESH,
            )
        )

    def begin(copies):
        for copy in copies:
            copy.start()

    early = me_g > 0

    arrive(2)
    for d in range(ndim):
        w_stiff[d * cp : d * cp + nb, :nb] = stiff[d]
    a_stiff = lanes3(-w_stiff[...], cp)
    many = 3 if nf % 3 == 0 else 1
    rows = ndim * cp

    def spread_out(fields):
        out = []
        for x in fields:
            high, low = halves(x)
            out.append(stacked([high, high, low], 128))
        return jnp.concatenate(out, axis=1)

    def mixed(turn, f):
        sums = [None] * many
        for g in range(nf):
            for d in range(ndim):
                x = parts[turn, g, d * cp : (d + 1) * cp]
                for m in range(many):
                    term = jac[f + m, g, pl.ds(d, 1), :] * x
                    sums[m] = term if sums[m] is None else sums[m] + term
        return sums

    arrive(0)
    for f in range(0, nf, many):
        group = [
            jnp.concatenate([dofs[f + m], jnp.zeros((cp - nb, elems), F32)], axis=0)
            for m in range(many)
        ]
        r = mul(a_stiff, spread_out(group))
        for m in range(many):
            integ[f + m] = group[m]
            parts[0, f + m] = r[:, m * elems : (m + 1) * elems]

    arrive(1)
    factorial = 1.0
    for degree in range(1, DERIV + 1):
        factorial = factorial * (degree + 1)
        turn = (degree - 1) % 2
        for f in range(0, nf, many):
            group = mixed(turn, f)
            for m in range(many):
                integ[f + m] = integ[f + m] + group[m] / factorial
            if degree < DERIV:
                r = mul(a_stiff, spread_out(group))
                for m in range(many):
                    parts[1 - turn, f + m] = r[:, m * elems : (m + 1) * elems]
        if degree == 2:
            arrive(16, 17)
            par_recv[:, here, :] = par[:, here, :]

            @pl.when(early)
            def _():
                pl.semaphore_wait(barrier, n_group + 1)
                begin(par_copies)

    arrive(10, 11, 13)
    for k in range(nface):
        for b in range(nb):
            w_ftrace[k, b : b + 1, :nq] = fault_trace[b, pl.ds(k, 1), :]
    lane = lax.broadcasted_iota(jnp.int32, (1, width), 1)
    is_v1 = (lane & slots) != 0
    sign_i = jnp.where((lane & (2 * slots)) != 0, 1.0, -1.0).astype(F32)
    slot_group = (lane & (slots - 1)) // CAP
    elem = fault_element[...]
    face = fault_face[...]
    elem_row = jnp.concatenate([elem[0:1], elem[0:1], elem[1:2], elem[1:2]], axis=1)
    face_row = jnp.concatenate([face[0:1], face[0:1], face[1:2], face[1:2]], axis=1)
    hit = lax.broadcasted_iota(jnp.int32, (elems, width), 0) == elem_row
    hot = jnp.where(hit, 1.0, 0.0).astype(F32)

    i0, i3, i7 = integ[0], integ[3], integ[7]
    highs, lows = zip(*[halves(x) for x in (i0, i3, i7)])
    g = mul(stacked(list(highs) + list(lows), 6 * cp), hot.astype(BF16))
    g = g[: 3 * cp] + g[3 * cp :]
    g0, g3, g7 = g[:cp], g[cp : 2 * cp], g[2 * cp :]
    a_fault = []
    for k in range(nface):
        high, low = halves(w_ftrace[k])
        gap = jnp.zeros((128 - 3 * cp, 128), F32)
        a_fault.append(jnp.concatenate([high, low, high, gap], axis=0).T[:qp])
    a_fault = jnp.concatenate(a_fault, axis=0).astype(BF16)

    def fault_sides(x):
        high, low = halves(x)
        y = mul(a_fault, stacked([high, high, low], 128))
        total = jnp.where(face_row == 0, y[:qp], 0.0)
        for k in range(1, nface):
            total = jnp.where(face_row == k, y[k * qp : (k + 1) * qp], total)
        return total

    mean = fault_sides(jnp.where(is_v1, 0.5 * g3 + (0.5 * sign_i) * g7, 0.5 * g0))
    mean = mean + roll(mean, 2 * slots)
    mean_t = jnp.concatenate([mean, jnp.zeros((128 - qp, width), F32)], axis=0).T
    normal_here = mean_t[:slots, :nq]
    locked_here = mean_t[slots : 2 * slots, :nq]
    fric_send[0] = normal_here
    fric_send[1] = locked_here
    sides = fault_sides(jnp.where(is_v1, g7, g3))
    fric_recv[:, here, :] = fric_send[:, here, :]

    @pl.when(early)
    def _():
        begin(fric_copies)

    arrive(3, 4)
    for k in range(nk):
        w_near[k * fp : k * fp + nfm, :nb] = neighbour_trace[k]
    for j in range(nj):
        for q in range(nfm):
            w_face[j * fp + q : j * fp + q + 1, :nb] = face_trace[q, pl.ds(j, 1), :]
    gap = jnp.zeros((128 - cp, 128), F32)
    v = [jnp.concatenate([w_stiff[d * cp : (d + 1) * cp], gap], axis=0).T[:cp] for d in range(ndim)]
    a_last = jnp.concatenate(
        [lanes3(jnp.concatenate(v, axis=0), cp), lanes3(w_face[...], cp)], axis=0
    )
    a_near = lanes3(w_near[...], cp)
    turn = DERIV % 2
    for f in range(0, nf, many):
        r = mul(a_last, spread_out([integ[f + m] for m in range(many)]))
        for m in range(many):
            y = r[:, m * elems : (m + 1) * elems]
            parts[turn, f + m] = y[:rows]
            y = y[rows:]
            for j in range(nj):
                own[j, f + m] = y[j * fp : (j + 1) * fp]

    arrive(8, 9)
    picked = [roll(rim[...], elems // 2)] + [code[j : j + 1, :] for j in range(1, nj)]
    maps, hots = [], []
    for row in picked:
        group = jnp.zeros_like(row)
        for k in range(1, nk):
            group = group + jnp.where(row >= k * elems, 1, 0)
        maps.append(group)
        hit = lax.broadcasted_iota(jnp.int32, (elems, elems), 0) == row - group * elems
        hots.append(jnp.where(hit, 1.0, 0.0).astype(F32))
    column = jnp.concatenate(hots, axis=1).astype(BF16)
    whole = jnp.concatenate([integ[f] for f in range(nf)], axis=0)
    high, low = halves(whole)
    tall = up(nf * cp, 16)
    gathered[...] = mul(
        jnp.concatenate([stacked([high], tall), stacked([low], tall)], axis=1),
        jnp.concatenate([column, column], axis=0),
    )

    def near_traces(i, store):
        which = jnp.broadcast_to(maps[i], (fp, elems))
        for f in range(0, nf, many):
            at = slice(i * elems, (i + 1) * elems)
            r = mul(
                a_near,
                spread_out([gathered[(f + m) * cp : (f + m + 1) * cp, at] for m in range(many)]),
            )
            for m in range(many):
                y = r[:, m * elems : (m + 1) * elems]
                total = y[:fp]
                for k in range(1, nk):
                    total = jnp.where(which == k, y[k * fp : (k + 1) * fp], total)
                store(f + m, total)

    def store_rim(f, total):
        rim_send[f] = total

    near_traces(0, store_rim)

    @pl.when(early)
    def _():
        begin(rim_copies)

    for j in range(1, nj):

        def store_near(f, total, j=j):
            near[j - 1, f] = total

        near_traces(j, store_near)

    for f in range(0, nf, many):
        group = mixed(turn, f)
        for m in range(many):
            base[f + m] = group[m]

    @pl.when(jnp.logical_not(early))
    def _():
        pl.semaphore_wait(barrier, n_group + 1)
        begin(par_copies + fric_copies + rim_copies)

    arrive(5, 6, 7)
    for j in range(nj):
        for q in range(nfm):
            w_lift[j * fp + q : j * fp + q + 1, :nb] = face_lift[q, pl.ds(j, 1), :]
    def face_flux(j, at_row, field):
        def step(i, carry):
            f = i * many
            sums = [None] * many
            for g in range(nf):
                mine, other = own[j, g], field(g)
                for m in range(many):
                    term = own_flux[f + m, g, pl.ds(j, 1), :] * mine
                    term = term + neighbour_flux[f + m, g, pl.ds(j, 1), :] * other
                    sums[m] = term if sums[m] is None else sums[m] + term
            for m in range(many):
                at = pl.ds(pl.multiple_of((f + m) * elems, elems), elems)
                flux[at_row : at_row + fp, at] = sums[m]
            return carry

        lax.fori_loop(0, nf // many, step, 0)

    kj = (nj - 1) * fp
    kr = up(kj, 16)
    for j in range(1, nj):
        face_flux(j, (j - 1) * fp, lambda g, j=j: near[j - 1, g])
    lift_all = w_lift[...].T[:cp]
    lift = roll(lift_all, 128 - fp)
    l_hi, l_lo = halves(lift)
    l_hi, l_lo = l_hi[:, :kr], l_lo[:, :kr]
    k_lane = lax.broadcasted_iota(jnp.int32, lift_all.shape, 1)
    x = flux[:kj]
    high, low = halves(x)
    x_hi = stacked([high], kr)
    r = mul(stacked([l_hi, l_lo], 2 * cp), x_hi)
    r = r[:cp] + r[cp:] + mul(l_hi.astype(BF16), stacked([low], kr))
    for f in range(nf):
        base[f] = base[f] - r[:, f * elems : (f + 1) * elems]

    for copy in par_copies:
        copy.wait_recv()
    slip = friction(normal_here, locked_here, par_recv[0], par_recv[1])
    signed = jnp.where(locked_here < 0.0, -slip, jnp.where(locked_here > 0.0, slip, 0.0))
    for i in range(4):
        slip_pad[i * slots : (i + 1) * slots, :nq] = signed

    arrive(12, 14, 15)
    for k in range(nface):
        for b in range(nb):
            w_flift[k * cp + b : k * cp + b + 1, :nq] = fault_lift[b, pl.ds(k, 1), :]
    live = jnp.zeros_like(lane)
    for o in range(n_group):
        live = jnp.where(slot_group == o, send_count[0, o], live)
    live = (lane & (CAP - 1)) < live
    side = jnp.where(live, face_row, -1)
    hot0 = jnp.where(is_v1, 0.0, hot)
    hot1 = jnp.where(is_v1, hot, 0.0)
    spread = stacked([hot0, hot1], 2 * elems)
    f_hi, f_lo = halves(w_flift[...])
    kq = 64
    a_lift = jnp.concatenate([f_hi + roll(f_lo, kq), f_hi], axis=1)[:, : 3 * kq].astype(BF16)
    turned = roll(mean, slots)
    locked = jnp.where(is_v1, mean, turned)
    drive_0 = jnp.where(is_v1, 0.5 * (roll(sides, 2 * slots) - sides), locked - sides)
    drive_1 = jnp.where(is_v1, 0.5 * sign_i, -1.0)
    answer = slip_pad[...].T[:qp]
    drive = drive_0 + drive_1 * answer
    high, low = halves(drive)
    gap = jnp.zeros((kq - qp, width), F32)
    y = mul(a_lift, stacked([high, gap, high, gap, low, gap], 3 * kq))
    lifted = jnp.where(side == 0, y[:cp], 0.0)
    for k in range(1, nface):
        lifted = jnp.where(side == k, y[k * cp : (k + 1) * cp], lifted)
    high, low = halves(lifted)
    z = lax.dot_general(
        stacked([high, low], 2 * cp),
        spread,
        (((1,), (1,)), ((), ())),
        preferred_element_type=F32,
    )
    z = z[:cp] + z[cp:]
    by_traction, by_jump = z[:, :elems], z[:, elems:]
    for copy in rim_copies:
        copy.wait_recv()
    e_lane = lax.broadcasted_iota(jnp.int32, (1, elems), 1)
    has_prev = jnp.where(me_s > 0, 1, 0)
    has_next = jnp.where(me_s < n_sub - 1, 1, 0)
    from_prev = (e_lane < elems // 2) & (has_prev == 1)
    from_next = (e_lane >= elems // 2) & (has_next == 1)
    for f in range(nf):
        near[0, f] = jnp.where(
            from_prev, rim_recv[0, f], jnp.where(from_next, rim_recv[1, f], 0.0)
        )
    face_flux(0, 0, lambda g: near[0, g])
    high, low = halves(flux[:fp])
    l0 = lanes3(jnp.where(k_lane < fp, lift_all, 0.0), fp)[:, : 3 * fp]
    r = mul(l0, stacked([high, high, low], 3 * fp))

    for f in range(nf):
        add = coupling[0, f] * by_traction + coupling[1, f] * by_jump
        total = base[f] - r[:, f * elems : (f + 1) * elems] + add
        out[f] = dofs[f] + total[:nb]


    arrive(18)
    for copy in fric_copies:
        copy.wait_recv()
    state = par[0]
    slip = friction(fric_recv[0], fric_recv[1], state, par[1])
    out_state[...] = state + 0.5 * evolution_rate[...] * (jnp.exp(-state) - slip)

    for copy in par_copies + fric_copies + rim_copies:
        copy.wait_send()


def finish(dofs, state, out, out_state, sem):
    copies = [
        pltpu.make_async_copy(dofs, out, sem.at[0]),
        pltpu.make_async_copy(state, out_state, sem.at[1]),
    ]
    for copy in copies:
        copy.start()
    for copy in copies:
        copy.wait()


def body(*args):
    args = list(args)
    n_group, n_sub = lax.axis_size("group"), lax.axis_size("sub")
    orders = {1: (1, 2, 0, 3), 3: (1, 0, 2), 5: (1, 2, 0, 3), 6: (1, 2, 0, 3), 7: (2, 0, 1)}
    orders |= {13: (2, 0, 1), 14: (1, 0, 2)}
    orders |= {i: (1, 0) for i in (12, 15, 16, 17, 18)}
    for i, order in orders.items():
        args[i] = jnp.transpose(args[i], order)
    nf, nb, elems = args[0].shape
    nfm, nj, _ = args[3].shape
    nk = args[4].shape[0]
    ndim = args[2].shape[0]
    _, nface, nq = args[13].shape
    slots = args[10].shape[1]
    args[9] = args[9].reshape(1, elems)
    cp, fp, qp = up(nb, 8), up(nfm, 8), up(nq, 8)
    width = 4 * slots
    vmem = pl.BlockSpec(memory_space=pltpu.VMEM)
    anywhere = pl.BlockSpec(memory_space=pl.ANY)
    held = [(pltpu.SMEM if i in (12, 15) else pltpu.VMEM)(a.shape, a.dtype) for i, a in enumerate(args)]
    shapes = (args[0].shape, args[16].shape)
    copies = 2 * (n_group - 1) + 2
    dofs, state = pl.pallas_call(
        functools.partial(kernel, n_group, n_sub),
        out_shape=tuple(pltpu.VMEM(s, F32) for s in shapes),
        in_specs=[anywhere] * len(args),
        out_specs=(vmem, vmem),
        scratch_shapes=held[:16]
        + held[18:]
        + [
            pltpu.VMEM((2,) + args[16].shape, F32),
            pltpu.VMEM((nf, cp, elems), F32),
            pltpu.VMEM((2, nf, ndim * cp, elems), F32),
            pltpu.VMEM((up(nf * cp, 16), nj * elems), F32),
            pltpu.VMEM((nj, nf, fp, elems), F32),
            pltpu.VMEM((nj, nf, fp, elems), F32),
            pltpu.VMEM((up((nj - 1) * fp, 16), nf * elems), F32),
            pltpu.VMEM((nf, cp, elems), F32),
            pltpu.VMEM((ndim * cp, 128), F32),
            pltpu.VMEM((nj * fp, 128), F32),
            pltpu.VMEM((nk * fp, 128), F32),
            pltpu.VMEM((nface, cp, 128), F32),
            pltpu.VMEM((nface * cp, 128), F32),
            pltpu.VMEM((128, 128), F32),
            pltpu.VMEM((nf, fp, elems), F32),
            pltpu.VMEM((2, nf, fp, elems), F32),
            pltpu.VMEM((2, slots, nq), F32),
            pltpu.VMEM((2, slots, nq), F32),
            pltpu.VMEM((2, slots, nq), F32),
            pltpu.VMEM((width, 128), F32),
            pltpu.SemaphoreType.DMA((len(args),)),
            pltpu.SemaphoreType.DMA((copies,)),
            pltpu.SemaphoreType.DMA((copies,)),
        ],
        compiler_params=pltpu.CompilerParams(collective_id=0, has_side_effects=True),
    )(*args)
    dofs, state = pl.pallas_call(
        finish,
        out_shape=tuple(jax.ShapeDtypeStruct(s, F32) for s in shapes),
        in_specs=[vmem, vmem],
        out_specs=(anywhere, anywhere),
        scratch_shapes=[pltpu.SemaphoreType.DMA((2,))],
        compiler_params=pltpu.CompilerParams(vmem_limit_bytes=8 << 20),
    )(dofs, state)
    return dofs, state.T


def solution(mesh):
    both = ("group", "sub")
    placed = (
        P(None, None, both),
        P(None, None, None, both),
        P(),
        P(),
        P(),
        P(None, None, None, both),
        P(None, None, None, both),
        P(),
        P(None, both),
        P(both),
        P(None, both),
        P(None, both),
        P(None, both),
        P(),
        P(),
        P(),
        P(None, both),
        P(None, both),
        P(None, both),
    )
    return jax.shard_map(
        body,
        mesh=mesh,
        in_specs=placed,
        out_specs=(P(None, None, both), P(None, both)),
        check_vma=False,
    )
```

```python
import functools

import jax
import jax.numpy as jnp
from jax import lax
from jax.experimental import pallas as pl
from jax.experimental.pallas import tpu as pltpu
from jax.sharding import PartitionSpec as P

DERIV = 4
NEWTON = 3
CAP = 8
F32 = jnp.float32
BF16 = jnp.bfloat16
MESH = pl.DeviceIdType.MESH


def up(n, m):
    return (n + m - 1) // m * m


def halves(x):
    high = x.astype(BF16).astype(F32)
    return high, x - high


def stacked(parts, rows):
    have = sum(p.shape[0] for p in parts)
    if have < rows:
        parts = parts + [jnp.zeros((rows - have, parts[0].shape[1]), F32)]
    return jnp.concatenate(parts, axis=0).astype(BF16)


def mul(a, b):
    return lax.dot_general(a, b, (((1,), (0,)), ((), ())), preferred_element_type=F32)


def roll(x, shift):
    return pltpu.roll(x, shift, 1)


def lanes3(a, step):
    high, low = halves(a)
    return (high + roll(low, step) + roll(high, 2 * step)).astype(BF16)


def friction(normal, locked, state, direct):
    rate = 0.5 * jnp.exp(state / direct)
    x = 2.0 - normal
    load = jnp.maximum(x, 0.0) + jnp.log1p(jnp.exp(-jnp.abs(x)))
    strength = load * direct
    magnitude = jnp.abs(locked)
    slip = magnitude / (1.0 + strength * rate)
    for _ in range(1, NEWTON):
        scaled = rate * slip
        root = jnp.sqrt(1.0 + scaled * scaled)
        log = jnp.log(jnp.abs(scaled) + root)
        log = jnp.where(scaled < 0.0, -log, log)
        slip = slip - (slip + strength * log - magnitude) / (1.0 + strength * rate / root)
    return slip


N_IN = 19
ORDER = (2, 0, 1, 13, 10, 11, 16, 17, 4, 3, 9, 8, 7, 14, 18, 12, 15, 5, 6)


def kernel(n_group, n_sub, *refs):
    hbm, out, out_state = refs[:N_IN], refs[N_IN], refs[N_IN + 1]
    local = refs[N_IN + 2 : 2 * N_IN]
    (
        par,
        integ,
        parts,
        gathered,
        own,
        near,
        flux,
        base,
        w_stiff,
        w_face,
        w_near,
        w_ftrace,
        w_flift,
        w_lift,
        rim_send,
        rim_recv,
        fric_send,
        fric_recv,
        par_send,
        par_recv,
        stage_sem,
        send_sem,
        recv_sem,
    ) = refs[2 * N_IN :]
    me_g = lax.axis_index("group")
    me_s = lax.axis_index("sub")
    has_prev = me_s > 0
    has_next = me_s < n_sub - 1
    barrier = pltpu.get_barrier_semaphore()
    for d in range(1, n_group):
        pl.semaphore_signal(
            barrier, inc=1, device_id=(lax.rem(me_g + d, n_group), me_s), device_id_type=MESH
        )
    for side, s in ((has_prev, me_s - 1), (has_next, me_s + 1)):

        @pl.when(side)
        def _(s=s):
            pl.semaphore_signal(barrier, inc=1, device_id=(me_g, s), device_id_type=MESH)

    greeted = n_group - 1 + jnp.where(has_prev, 1, 0) + jnp.where(has_next, 1, 0)

    held = list(local[:16]) + [par.at[0], par.at[1]] + list(local[16:])
    staged = {i: pltpu.make_async_copy(hbm[i], held[i], stage_sem.at[i]) for i in ORDER}
    for i in ORDER:
        staged[i].start()

    def arrive(*which):
        for i in which:
            staged[i].wait()

    (
        dofs,
        jac,
        stiff,
        face_trace,
        neighbour_trace,
        own_flux,
        neighbour_flux,
        face_lift,
        code,
        rim,
        fault_element,
        fault_face,
        send_count,
        fault_trace,
        fault_lift,
        coupling,
    ) = held[:16]
    evolution_rate = held[18]
    nf, nb, elems = dofs.shape
    ndim = stiff.shape[0]
    nfm, nj, _ = face_trace.shape
    nk = neighbour_trace.shape[0]
    _, nface, nq = fault_trace.shape
    slots = fault_element.shape[1]
    cp, fp, qp = up(nb, 8), up(nfm, 8), up(nq, 8)
    width = 4 * slots

    w_stiff[...] = jnp.zeros_like(w_stiff)
    w_ftrace[...] = jnp.zeros_like(w_ftrace)
    w_face[...] = jnp.zeros_like(w_face)
    w_near[...] = jnp.zeros_like(w_near)
    w_flift[...] = jnp.zeros_like(w_flift)
    w_lift[...] = jnp.zeros_like(w_lift)
    par_send[...] = jnp.ones_like(par_send)

    def to_group(src, dst, first):
        copies = []
        for d in range(1, n_group):
            o = lax.rem(me_g + d, n_group)
            copies.append(
                pltpu.make_async_remote_copy(
                    src_ref=src.at[o],
                    dst_ref=dst.at[me_g],
                    send_sem=send_sem.at[first + d - 1],
                    recv_sem=recv_sem.at[first + d - 1],
                    device_id=(o, me_s),
                    device_id_type=MESH,
                )
            )
        return copies

    par_copies = to_group(par_send, par_recv, 0)
    fric_copies = to_group(fric_send, fric_recv, n_group - 1)
    rim_copies = []
    for side, s in enumerate((me_s + 1, me_s - 1)):
        rim_copies.append(
            pltpu.make_async_remote_copy(
                src_ref=rim_send.at[side],
                dst_ref=rim_recv.at[side],
                send_sem=send_sem.at[2 * (n_group - 1) + side],
                recv_sem=recv_sem.at[2 * (n_group - 1) + side],
                device_id=(me_g, s),
                device_id_type=MESH,
            )
        )

    def begin(copies):
        for copy in copies:
            copy.start()

    def begin_rim():
        for copy, there in zip(rim_copies, (has_next, has_prev)):
            pl.when(there)(copy.start)

    first_row = me_g == 0
    corner = first_row & (me_s == 0)

    arrive(2)
    for d in range(ndim):
        w_stiff[d * cp : d * cp + nb, :nb] = stiff[d]
    a_stiff = lanes3(-w_stiff[...], cp)
    many = 3 if nf % 3 == 0 else 1
    rows = ndim * cp

    def spread_out(fields):
        out = []
        for x in fields:
            high, low = halves(x)
            out.append(stacked([high, high, low], 128))
        return jnp.concatenate(out, axis=1)

    def mixed(turn, fields):
        sums = [None] * len(fields)
        for g in range(nf):
            for d in range(ndim):
                x = parts[turn, g, d * cp : (d + 1) * cp]
                for m, f in enumerate(fields):
                    term = jac[f, g, pl.ds(d, 1), :] * x
                    sums[m] = term if sums[m] is None else sums[m] + term
        return sums

    arrive(0)
    for f in range(0, nf, many):
        group = [
            jnp.concatenate([dofs[f + m], jnp.zeros((cp - nb, elems), F32)], axis=0)
            for m in range(many)
        ]
        r = mul(a_stiff, spread_out(group))
        for m in range(many):
            integ[f + m] = group[m]
            parts[0, f + m] = r[:, m * elems : (m + 1) * elems]

    arrive(1)
    arrive(10, 11, 13)
    for k in range(nface):
        for b in range(nb):
            w_ftrace[k, b : b + 1, :nq] = fault_trace[b, pl.ds(k, 1), :]
    lane = lax.broadcasted_iota(jnp.int32, (1, width), 1)
    is_v1 = (lane & slots) != 0
    sign_i = jnp.where((lane & (2 * slots)) != 0, 1.0, -1.0).astype(F32)
    slot_group = (lane & (slots - 1)) // CAP
    elem = fault_element[...]
    face = fault_face[...]
    elem_row = jnp.concatenate([elem[0:1], elem[0:1], elem[1:2], elem[1:2]], axis=1)
    face_row = jnp.concatenate([face[0:1], face[0:1], face[1:2], face[1:2]], axis=1)
    hit = lax.broadcasted_iota(jnp.int32, (elems, width), 0) == elem_row
    hot = jnp.where(hit, 1.0, 0.0).astype(F32)

    a_fault = []
    for k in range(nface):
        high, low = halves(w_ftrace[k])
        gap = jnp.zeros((128 - 3 * cp, 128), F32)
        a_fault.append(jnp.concatenate([high, low, high, gap], axis=0).T[:qp])
    a_fault = jnp.concatenate(a_fault, axis=0).astype(BF16)

    factorial = 1.0
    for degree in range(1, DERIV):
        factorial = factorial * (degree + 1)
        turn = (degree - 1) % 2
        for f in range(0, nf, many):
            group = mixed(turn, range(f, f + many))
            for m in range(many):
                integ[f + m] = integ[f + m] + group[m] / factorial
            r = mul(a_stiff, spread_out(group))
            for m in range(many):
                parts[1 - turn, f + m] = r[:, m * elems : (m + 1) * elems]
        if degree == 2:
            arrive(16, 17)
            for o in range(n_group):
                for i in range(2):
                    par_send[o, i, :, :nq] = par[i, o * CAP : (o + 1) * CAP, :]
            par_recv[me_g] = par_send[me_g]

            @pl.when(jnp.logical_not(first_row))
            def _():
                pl.semaphore_wait(barrier, greeted)
                begin(par_copies)

    factorial = factorial * (DERIV + 1)

    def finished(fields):
        for f, x in zip(fields, mixed((DERIV - 1) % 2, fields)):
            integ[f] = integ[f] + x / factorial

    picked = (0, 3, 7)
    finished(picked)

    i0, i3, i7 = integ[0], integ[3], integ[7]
    highs, lows = zip(*[halves(x) for x in (i0, i3, i7)])
    g = mul(stacked(list(highs) + list(lows), 6 * cp), hot.astype(BF16))
    g = g[: 3 * cp] + g[3 * cp :]
    g0, g3, g7 = g[:cp], g[cp : 2 * cp], g[2 * cp :]
    def fault_sides(x):
        high, low = halves(x)
        y = mul(a_fault, stacked([high, high, low], 128))
        total = jnp.where(face_row == 0, y[:qp], 0.0)
        for k in range(1, nface):
            total = jnp.where(face_row == k, y[k * qp : (k + 1) * qp], total)
        return total

    mean = fault_sides(jnp.where(is_v1, 0.5 * g3 + (0.5 * sign_i) * g7, 0.5 * g0))
    mean = mean + roll(mean, 2 * slots)
    mean_t = jnp.concatenate([mean, jnp.zeros((128 - qp, width), F32)], axis=0).T
    normal_here = mean_t[:slots]
    locked_here = mean_t[slots : 2 * slots]
    for o in range(n_group):
        fric_send[o, 0] = normal_here[o * CAP : (o + 1) * CAP]
        fric_send[o, 1] = locked_here[o * CAP : (o + 1) * CAP]
    fric_recv[me_g] = fric_send[me_g]

    @pl.when(jnp.logical_not(first_row))
    def _():
        begin(fric_copies)

    @pl.when(first_row & (me_s > 0))
    def _():
        pl.semaphore_wait(barrier, greeted)
        begin(par_copies + fric_copies)

    sides = fault_sides(jnp.where(is_v1, g7, g3))
    rest = [f for f in range(nf) if f not in picked]
    for i in range(0, len(rest), many):
        finished(rest[i : i + many])

    arrive(3, 4)
    for k in range(nk):
        w_near[k * fp : k * fp + nfm, :nb] = neighbour_trace[k]
    for j in range(nj):
        for q in range(nfm):
            w_face[j * fp + q : j * fp + q + 1, :nb] = face_trace[q, pl.ds(j, 1), :]
    gap = jnp.zeros((128 - cp, 128), F32)
    v = [jnp.concatenate([w_stiff[d * cp : (d + 1) * cp], gap], axis=0).T[:cp] for d in range(ndim)]
    a_last = jnp.concatenate(
        [lanes3(jnp.concatenate(v, axis=0), cp), lanes3(w_face[...], cp)], axis=0
    )
    a_near = lanes3(w_near[...], cp)
    turn = DERIV % 2
    for f in range(0, nf, many):
        r = mul(a_last, spread_out([integ[f + m] for m in range(many)]))
        for m in range(many):
            y = r[:, m * elems : (m + 1) * elems]
            parts[turn, f + m] = y[:rows]
            y = y[rows:]
            for j in range(nj):
                own[j, f + m] = y[j * fp : (j + 1) * fp]

    arrive(8, 9)
    lists = [roll(rim[...], elems // 2)] + [code[j : j + 1, :] for j in range(1, nj)]
    maps, hots = [], []
    for row in lists:
        group = jnp.zeros_like(row)
        for k in range(1, nk):
            group = group + jnp.where(row >= k * elems, 1, 0)
        maps.append(group)
        hit = lax.broadcasted_iota(jnp.int32, (elems, elems), 0) == row - group * elems
        hots.append(jnp.where(hit, 1.0, 0.0).astype(F32))
    column = jnp.concatenate(hots, axis=1).astype(BF16)
    whole = jnp.concatenate([integ[f] for f in range(nf)], axis=0)
    high, low = halves(whole)
    tall = up(nf * cp, 16)
    gathered[...] = mul(
        jnp.concatenate([stacked([high], tall), stacked([low], tall)], axis=1),
        jnp.concatenate([column, column], axis=0),
    )

    def near_traces(i, store):
        which = jnp.broadcast_to(maps[i], (fp, elems))
        for f in range(0, nf, many):
            at = slice(i * elems, (i + 1) * elems)
            r = mul(
                a_near,
                spread_out([gathered[(f + m) * cp : (f + m + 1) * cp, at] for m in range(many)]),
            )
            for m in range(many):
                y = r[:, m * elems : (m + 1) * elems]
                total = y[:fp]
                for k in range(1, nk):
                    total = jnp.where(which == k, y[k * fp : (k + 1) * fp], total)
                store(f + m, total)

    e_lane = lax.broadcasted_iota(jnp.int32, (1, elems), 1)
    lower = e_lane < elems // 2
    fh = fp // 2

    def store_rim(f, total):
        top, turned = total[:fh], roll(total[fh:], elems // 2)
        rim_send[0, f] = jnp.where(lower, top, turned)
        rim_send[1, f] = jnp.where(lower, turned, top)

    near_traces(0, store_rim)

    @pl.when(jnp.logical_not(corner))
    def _():
        begin_rim()

    for j in range(1, nj):

        def store_near(f, total, j=j):
            near[j - 1, f] = total

        near_traces(j, store_near)

    for f in range(0, nf, many):
        group = mixed(turn, range(f, f + many))
        for m in range(many):
            base[f + m] = group[m]

    @pl.when(corner)
    def _():
        pl.semaphore_wait(barrier, greeted)
        begin(par_copies + fric_copies)
        begin_rim()

    arrive(5, 6, 7)
    for j in range(nj):
        for q in range(nfm):
            w_lift[j * fp + q : j * fp + q + 1, :nb] = face_lift[q, pl.ds(j, 1), :]
    def face_flux(j, at_row, field):
        def step(i, carry):
            f = i * many
            sums = [None] * many
            for g in range(nf):
                mine, other = own[j, g], field(g)
                for m in range(many):
                    term = own_flux[f + m, g, pl.ds(j, 1), :] * mine
                    term = term + neighbour_flux[f + m, g, pl.ds(j, 1), :] * other
                    sums[m] = term if sums[m] is None else sums[m] + term
            for m in range(many):
                at = pl.ds(pl.multiple_of((f + m) * elems, elems), elems)
                flux[at_row : at_row + fp, at] = sums[m]
            return carry

        lax.fori_loop(0, nf // many, step, 0)

    kj = (nj - 1) * fp
    kr = up(kj, 16)
    for j in range(1, nj):
        face_flux(j, (j - 1) * fp, lambda g, j=j: near[j - 1, g])
    lift_all = w_lift[...].T[:cp]
    lift = roll(lift_all, 128 - fp)
    l_hi, l_lo = halves(lift)
    l_hi, l_lo = l_hi[:, :kr], l_lo[:, :kr]
    k_lane = lax.broadcasted_iota(jnp.int32, lift_all.shape, 1)
    x = flux[:kj]
    high, low = halves(x)
    x_hi = stacked([high], kr)
    r = mul(stacked([l_hi, l_lo], 2 * cp), x_hi)
    r = r[:cp] + r[cp:] + mul(l_hi.astype(BF16), stacked([low], kr))
    for f in range(nf):
        base[f] = base[f] - r[:, f * elems : (f + 1) * elems]

    for copy in par_copies:
        copy.wait_recv()
    state = par_recv[:, 0].reshape(slots, 128)
    slip = friction(normal_here, locked_here, state, par_recv[:, 1].reshape(slots, 128))
    signed = jnp.where(locked_here < 0.0, -slip, jnp.where(locked_here > 0.0, slip, 0.0))
    point = lax.broadcasted_iota(jnp.int32, (1, 128), 1)
    signed = jnp.where(point < nq, signed, 0.0)

    arrive(12, 14, 15)
    for k in range(nface):
        for b in range(nb):
            w_flift[k * cp + b : k * cp + b + 1, :nq] = fault_lift[b, pl.ds(k, 1), :]
    live = jnp.zeros_like(lane)
    for o in range(n_group):
        live = jnp.where(slot_group == o, send_count[0, o], live)
    live = (lane & (CAP - 1)) < live
    side = jnp.where(live, face_row, -1)
    hot0 = jnp.where(is_v1, 0.0, hot)
    hot1 = jnp.where(is_v1, hot, 0.0)
    spread = stacked([hot0, hot1], 2 * elems)
    f_hi, f_lo = halves(w_flift[...])
    kq = 64
    a_lift = jnp.concatenate([f_hi + roll(f_lo, kq), f_hi], axis=1)[:, : 3 * kq].astype(BF16)
    turned = roll(mean, slots)
    locked = jnp.where(is_v1, mean, turned)
    drive_0 = jnp.where(is_v1, 0.5 * (roll(sides, 2 * slots) - sides), locked - sides)
    drive_1 = jnp.where(is_v1, 0.5 * sign_i, -1.0)
    answer = jnp.concatenate([signed] * 4, axis=0).T[:qp]
    drive = drive_0 + drive_1 * answer
    high, low = halves(drive)
    gap = jnp.zeros((kq - qp, width), F32)
    y = mul(a_lift, stacked([high, gap, high, gap, low, gap], 3 * kq))
    lifted = jnp.where(side == 0, y[:cp], 0.0)
    for k in range(1, nface):
        lifted = jnp.where(side == k, y[k * cp : (k + 1) * cp], lifted)
    high, low = halves(lifted)
    z = lax.dot_general(
        stacked([high, low], 2 * cp),
        spread,
        (((1,), (1,)), ((), ())),
        preferred_element_type=F32,
    )
    z = z[:cp] + z[cp:]
    by_traction, by_jump = z[:, :elems], z[:, elems:]
    for copy, there in zip(rim_copies, (has_prev, has_next)):
        pl.when(there)(copy.wait_recv)
    from_prev = lower & has_prev
    from_next = jnp.logical_not(lower) & has_next
    for f in range(nf):
        x, y = rim_recv[0, f], rim_recv[1, f]
        for i, (x, y) in enumerate(((x, y), (roll(x, elems // 2), roll(y, elems // 2)))):
            near[0, f, i * fh : (i + 1) * fh] = jnp.where(from_prev, x, jnp.where(from_next, y, 0.0))
    face_flux(0, 0, lambda g: near[0, g])
    high, low = halves(flux[:fp])
    l0 = lanes3(jnp.where(k_lane < fp, lift_all, 0.0), fp)[:, : 3 * fp]
    r = mul(l0, stacked([high, high, low], 3 * fp))

    for f in range(nf):
        add = coupling[0, f] * by_traction + coupling[1, f] * by_jump
        total = base[f] - r[:, f * elems : (f + 1) * elems] + add
        out[f] = dofs[f] + total[:nb]


    arrive(18)
    for copy in fric_copies:
        copy.wait_recv()
    state = par[0]
    slip = friction(
        fric_recv[:, 0].reshape(slots, 128)[:, :nq],
        fric_recv[:, 1].reshape(slots, 128)[:, :nq],
        state,
        par[1],
    )
    out_state[...] = state + 0.5 * evolution_rate[...] * (jnp.exp(-state) - slip)

    for copy in par_copies + fric_copies:
        copy.wait_send()
    for copy, there in zip(rim_copies, (has_next, has_prev)):
        pl.when(there)(copy.wait_send)


def finish(dofs, state, out, out_state, sem):
    copies = [
        pltpu.make_async_copy(dofs, out, sem.at[0]),
        pltpu.make_async_copy(state, out_state, sem.at[1]),
    ]
    for copy in copies:
        copy.start()
    for copy in copies:
        copy.wait()


def body(*args):
    args = list(args)
    n_group, n_sub = lax.axis_size("group"), lax.axis_size("sub")
    orders = {1: (1, 2, 0, 3), 3: (1, 0, 2), 5: (1, 2, 0, 3), 6: (1, 2, 0, 3), 7: (2, 0, 1)}
    orders |= {13: (2, 0, 1), 14: (1, 0, 2)}
    orders |= {i: (1, 0) for i in (12, 15, 16, 17, 18)}
    for i, order in orders.items():
        args[i] = jnp.transpose(args[i], order)
    nf, nb, elems = args[0].shape
    nfm, nj, _ = args[3].shape
    nk = args[4].shape[0]
    ndim = args[2].shape[0]
    _, nface, nq = args[13].shape
    slots = args[10].shape[1]
    args[9] = args[9].reshape(1, elems)
    cp, fp, qp = up(nb, 8), up(nfm, 8), up(nq, 8)
    width = 4 * slots
    vmem = pl.BlockSpec(memory_space=pltpu.VMEM)
    anywhere = pl.BlockSpec(memory_space=pl.ANY)
    held = [(pltpu.SMEM if i in (12, 15) else pltpu.VMEM)(a.shape, a.dtype) for i, a in enumerate(args)]
    shapes = (args[0].shape, args[16].shape)
    copies = 2 * (n_group - 1) + 2
    dofs, state = pl.pallas_call(
        functools.partial(kernel, n_group, n_sub),
        out_shape=tuple(pltpu.VMEM(s, F32) for s in shapes),
        in_specs=[anywhere] * len(args),
        out_specs=(vmem, vmem),
        scratch_shapes=held[:16]
        + held[18:]
        + [
            pltpu.VMEM((2,) + args[16].shape, F32),
            pltpu.VMEM((nf, cp, elems), F32),
            pltpu.VMEM((2, nf, ndim * cp, elems), F32),
            pltpu.VMEM((up(nf * cp, 16), nj * elems), F32),
            pltpu.VMEM((nj, nf, fp, elems), F32),
            pltpu.VMEM((nj, nf, fp, elems), F32),
            pltpu.VMEM((up((nj - 1) * fp, 16), nf * elems), F32),
            pltpu.VMEM((nf, cp, elems), F32),
            pltpu.VMEM((ndim * cp, 128), F32),
            pltpu.VMEM((nj * fp, 128), F32),
            pltpu.VMEM((nk * fp, 128), F32),
            pltpu.VMEM((nface, cp, 128), F32),
            pltpu.VMEM((nface * cp, 128), F32),
            pltpu.VMEM((128, 128), F32),
            pltpu.VMEM((2, nf, fp // 2, elems), F32),
            pltpu.VMEM((2, nf, fp // 2, elems), F32),
        ]
        + [pltpu.VMEM((n_group, 2, CAP, 128), F32)] * 4
        + [
            pltpu.SemaphoreType.DMA((len(args),)),
            pltpu.SemaphoreType.DMA((copies,)),
            pltpu.SemaphoreType.DMA((copies,)),
        ],
        compiler_params=pltpu.CompilerParams(collective_id=0, has_side_effects=True),
    )(*args)
    dofs, state = pl.pallas_call(
        finish,
        out_shape=tuple(jax.ShapeDtypeStruct(s, F32) for s in shapes),
        in_specs=[vmem, vmem],
        out_specs=(anywhere, anywhere),
        scratch_shapes=[pltpu.SemaphoreType.DMA((2,))],
        compiler_params=pltpu.CompilerParams(vmem_limit_bytes=8 << 20),
    )(dofs, state)
    return dofs, state.T


def solution(mesh):
    both = ("group", "sub")
    placed = (
        P(None, None, both),
        P(None, None, None, both),
        P(),
        P(),
        P(),
        P(None, None, None, both),
        P(None, None, None, both),
        P(),
        P(None, both),
        P(both),
        P(None, both),
        P(None, both),
        P(None, both),
        P(),
        P(),
        P(),
        P(None, both),
        P(None, both),
        P(None, both),
    )
    return jax.shard_map(
        body,
        mesh=mesh,
        in_specs=placed,
        out_specs=(P(None, None, both), P(None, both)),
        check_vma=False,
    )
```

```python
import functools

import jax
import jax.numpy as jnp
from jax import lax
from jax.experimental import pallas as pl
from jax.experimental.pallas import tpu as pltpu
from jax.sharding import PartitionSpec as P

DERIV = 4
NEWTON = 3
CAP = 8
F32 = jnp.float32
BF16 = jnp.bfloat16
MESH = pl.DeviceIdType.MESH


def up(n, m):
    return (n + m - 1) // m * m


def halves(x):
    high = x.astype(BF16).astype(F32)
    return high, x - high


def stacked(parts, rows):
    have = sum(p.shape[0] for p in parts)
    if have < rows:
        parts = parts + [jnp.zeros((rows - have, parts[0].shape[1]), F32)]
    return jnp.concatenate(parts, axis=0).astype(BF16)


def mul(a, b):
    return lax.dot_general(a, b, (((1,), (0,)), ((), ())), preferred_element_type=F32)


def roll(x, shift):
    return pltpu.roll(x, shift, 1)


def lanes3(a, step):
    high, low = halves(a)
    return (high + roll(low, step) + roll(high, 2 * step)).astype(BF16)


def friction(normal, locked, state, direct):
    rate = 0.5 * jnp.exp(state / direct)
    x = 2.0 - normal
    load = jnp.maximum(x, 0.0) + jnp.log1p(jnp.exp(-jnp.abs(x)))
    strength = load * direct
    magnitude = jnp.abs(locked)
    slip = magnitude / (1.0 + strength * rate)
    for _ in range(1, NEWTON):
        scaled = rate * slip
        root = jnp.sqrt(1.0 + scaled * scaled)
        log = jnp.log(jnp.abs(scaled) + root)
        log = jnp.where(scaled < 0.0, -log, log)
        slip = slip - (slip + strength * log - magnitude) / (1.0 + strength * rate / root)
    return slip


N_IN = 19
ORDER = (2, 0, 1, 13, 10, 11, 16, 17, 4, 3, 9, 8, 7, 14, 18, 12, 15, 5, 6)

TOGETHER = ((2,), (0,), (1,), (10, 11, 13, 16, 17), (3, 4, 8, 9), (5, 6, 7), (12, 14, 15, 18))
SEM = {i: n for n, members in enumerate(TOGETHER) for i in members}


def kernel(n_group, n_sub, *refs):
    hbm, out, out_state = refs[:N_IN], refs[N_IN], refs[N_IN + 1]
    local = refs[N_IN + 2 : 2 * N_IN]
    (
        par,
        integ,
        parts,
        gathered,
        own,
        near,
        flux,
        base,
        w_stiff,
        w_face,
        w_near,
        w_ftrace,
        w_flift,
        w_lift,
        rim_send,
        rim_recv,
        fric_send,
        fric_recv,
        par_send,
        par_recv,
        stage_sem,
        send_sem,
        recv_sem,
    ) = refs[2 * N_IN :]
    me_g = lax.axis_index("group")
    me_s = lax.axis_index("sub")
    has_prev = me_s > 0
    has_next = me_s < n_sub - 1
    barrier = pltpu.get_barrier_semaphore()
    for d in range(1, n_group):
        pl.semaphore_signal(
            barrier, inc=1, device_id=(lax.rem(me_g + d, n_group), me_s), device_id_type=MESH
        )
    for side, s in ((has_prev, me_s - 1), (has_next, me_s + 1)):

        @pl.when(side)
        def _(s=s):
            pl.semaphore_signal(barrier, inc=1, device_id=(me_g, s), device_id_type=MESH)

    greeted = n_group - 1 + jnp.where(has_prev, 1, 0) + jnp.where(has_next, 1, 0)

    held = list(local[:16]) + [par.at[0], par.at[1]] + list(local[16:])
    staged = {i: pltpu.make_async_copy(hbm[i], held[i], stage_sem.at[SEM[i]]) for i in ORDER}
    for i in ORDER:
        staged[i].start()

    def arrive(*which):
        for i in which:
            staged[i].wait()

    (
        dofs,
        jac,
        stiff,
        face_trace,
        neighbour_trace,
        own_flux,
        neighbour_flux,
        face_lift,
        code,
        rim,
        fault_element,
        fault_face,
        send_count,
        fault_trace,
        fault_lift,
        coupling,
    ) = held[:16]
    evolution_rate = held[18]
    nf, nb, elems = dofs.shape
    ndim = stiff.shape[0]
    nfm, nj, _ = face_trace.shape
    nk = neighbour_trace.shape[0]
    _, nface, nq = fault_trace.shape
    slots = fault_element.shape[1]
    cp, fp, qp = up(nb, 8), up(nfm, 8), up(nq, 8)
    width = 4 * slots

    w_stiff[...] = jnp.zeros_like(w_stiff)
    w_ftrace[...] = jnp.zeros_like(w_ftrace)
    w_face[...] = jnp.zeros_like(w_face)
    w_near[...] = jnp.zeros_like(w_near)
    w_flift[...] = jnp.zeros_like(w_flift)
    w_lift[...] = jnp.zeros_like(w_lift)
    par_send[...] = jnp.ones_like(par_send)

    def to_group(src, dst, first):
        copies = []
        for d in range(1, n_group):
            o = lax.rem(me_g + d, n_group)
            copies.append(
                pltpu.make_async_remote_copy(
                    src_ref=src.at[o],
                    dst_ref=dst.at[me_g],
                    send_sem=send_sem.at[first + d - 1],
                    recv_sem=recv_sem.at[first + d - 1],
                    device_id=(o, me_s),
                    device_id_type=MESH,
                )
            )
        return copies

    par_copies = to_group(par_send, par_recv, 0)
    fric_copies = to_group(fric_send, fric_recv, n_group - 1)
    rim_copies = []
    for side, s in enumerate((me_s + 1, me_s - 1)):
        rim_copies.append(
            pltpu.make_async_remote_copy(
                src_ref=rim_send.at[side],
                dst_ref=rim_recv.at[side],
                send_sem=send_sem.at[2 * (n_group - 1) + side],
                recv_sem=recv_sem.at[2 * (n_group - 1) + side],
                device_id=(me_g, s),
                device_id_type=MESH,
            )
        )

    def begin(copies):
        for copy in copies:
            copy.start()

    def begin_rim():
        for copy, there in zip(rim_copies, (has_next, has_prev)):
            pl.when(there)(copy.start)

    first_row = me_g == 0
    far = me_g >= max(n_group // 2, 1)
    middle = jnp.logical_not(first_row | far)
    corner = first_row & (me_s == 0)

    arrive(2)
    for d in range(ndim):
        w_stiff[d * cp : d * cp + nb, :nb] = stiff[d]
    a_stiff = lanes3(-w_stiff[...], cp)
    many = 3 if nf % 3 == 0 else 1
    rows = ndim * cp

    def spread_out(fields):
        out = []
        for x in fields:
            high, low = halves(x)
            out.append(stacked([high, high, low], 128))
        return jnp.concatenate(out, axis=1)

    def mixed(turn, fields):
        sums = [None] * len(fields)
        for g in range(nf):
            for d in range(ndim):
                x = parts[turn, g, d * cp : (d + 1) * cp]
                for m, f in enumerate(fields):
                    term = jac[f, g, pl.ds(d, 1), :] * x
                    sums[m] = term if sums[m] is None else sums[m] + term
        return sums

    arrive(0)
    for f in range(0, nf, many):
        group = [
            jnp.concatenate([dofs[f + m], jnp.zeros((cp - nb, elems), F32)], axis=0)
            for m in range(many)
        ]
        r = mul(a_stiff, spread_out(group))
        for m in range(many):
            integ[f + m] = group[m]
            parts[0, f + m] = r[:, m * elems : (m + 1) * elems]

    arrive(1)
    arrive(10, 11, 13, 16, 17)
    for o in range(n_group):
        for i in range(2):
            par_send[o, i, :, :nq] = par[i, o * CAP : (o + 1) * CAP, :]
    par_recv[me_g] = par_send[me_g]

    @pl.when(far)
    def _():
        pl.semaphore_wait(barrier, greeted)
        begin(par_copies)

    for k in range(nface):
        for b in range(nb):
            w_ftrace[k, b : b + 1, :nq] = fault_trace[b, pl.ds(k, 1), :]
    lane = lax.broadcasted_iota(jnp.int32, (1, width), 1)
    is_v1 = (lane & slots) != 0
    sign_i = jnp.where((lane & (2 * slots)) != 0, 1.0, -1.0).astype(F32)
    slot_group = (lane & (slots - 1)) // CAP
    elem = fault_element[...]
    face = fault_face[...]
    elem_row = jnp.concatenate([elem[0:1], elem[0:1], elem[1:2], elem[1:2]], axis=1)
    face_row = jnp.concatenate([face[0:1], face[0:1], face[1:2], face[1:2]], axis=1)
    hit = lax.broadcasted_iota(jnp.int32, (elems, width), 0) == elem_row
    hot = jnp.where(hit, 1.0, 0.0).astype(F32)

    a_fault = []
    for k in range(nface):
        high, low = halves(w_ftrace[k])
        gap = jnp.zeros((128 - 3 * cp, 128), F32)
        a_fault.append(jnp.concatenate([high, low, high, gap], axis=0).T[:qp])
    a_fault = jnp.concatenate(a_fault, axis=0).astype(BF16)

    half_hot = 0.5 * hot
    weights = (
        jnp.where(is_v1, 0.0, half_hot),
        jnp.where(is_v1, half_hot, 0.0),
        jnp.where(is_v1, sign_i * half_hot, 0.0),
    )
    mixing = jnp.concatenate([w for w in weights for _ in range(2)], axis=0).astype(BF16)
    hot_16 = hot.astype(BF16)
    factorial = 1.0
    for degree in range(1, DERIV):
        factorial = factorial * (degree + 1)
        turn = (degree - 1) % 2
        for f in range(0, nf, many):
            group = mixed(turn, range(f, f + many))
            for m in range(many):
                integ[f + m] = integ[f + m] + group[m] / factorial
            r = mul(a_stiff, spread_out(group))
            for m in range(many):
                parts[1 - turn, f + m] = r[:, m * elems : (m + 1) * elems]
        if degree == 2:
            @pl.when(middle)
            def _():
                pl.semaphore_wait(barrier, greeted)
                begin(par_copies)

    factorial = factorial * (DERIV + 1)

    def finished(fields):
        for f, x in zip(fields, mixed((DERIV - 1) % 2, fields)):
            integ[f] = integ[f] + x / factorial

    picked = (0, 3, 7)
    finished(picked)

    def fault_sides(x):
        high, low = halves(x)
        y = mul(a_fault, stacked([high, high, low], 128))
        total = jnp.where(face_row == 0, y[:qp], 0.0)
        for k in range(1, nface):
            total = jnp.where(face_row == k, y[k * qp : (k + 1) * qp], total)
        return total

    tall = up(cp, 16)
    split = [stacked([p], tall) for f in picked for p in halves(integ[f])]
    mean = fault_sides(mul(jnp.concatenate(split, axis=1), mixing)[:cp])
    mean = mean + roll(mean, 2 * slots)
    mean_t = jnp.concatenate([mean, jnp.zeros((128 - qp, width), F32)], axis=0).T
    normal_here = mean_t[:slots]
    locked_here = mean_t[slots : 2 * slots]
    for o in range(n_group):
        fric_send[o, 0] = normal_here[o * CAP : (o + 1) * CAP]
        fric_send[o, 1] = locked_here[o * CAP : (o + 1) * CAP]
    fric_recv[me_g] = fric_send[me_g]

    @pl.when(jnp.logical_not(first_row))
    def _():
        begin(fric_copies)

    @pl.when(first_row & (me_s > 0))
    def _():
        pl.semaphore_wait(barrier, greeted)
        begin(par_copies + fric_copies)

    highs, lows = zip(*[halves(integ[f]) for f in picked[1:]])
    g = mul(stacked(list(highs) + list(lows), 4 * cp), hot_16)
    g = g[: 2 * cp] + g[2 * cp :]
    sides = fault_sides(jnp.where(is_v1, g[cp:], g[:cp]))
    rest = [f for f in range(nf) if f not in picked]
    for i in range(0, len(rest), many):
        finished(rest[i : i + many])

    arrive(3, 4, 8, 9)
    for k in range(nk):
        w_near[k * fp : k * fp + nfm, :nb] = neighbour_trace[k]
    for j in range(nj):
        for q in range(nfm):
            w_face[j * fp + q : j * fp + q + 1, :nb] = face_trace[q, pl.ds(j, 1), :]
    gap = jnp.zeros((128 - cp, 128), F32)
    v = [jnp.concatenate([w_stiff[d * cp : (d + 1) * cp], gap], axis=0).T[:cp] for d in range(ndim)]
    a_last = jnp.concatenate(
        [lanes3(jnp.concatenate(v, axis=0), cp), lanes3(w_face[...], cp)], axis=0
    )
    a_near = lanes3(w_near[...], cp)
    turn = DERIV % 2
    for f in range(0, nf, many):
        r = mul(a_last, spread_out([integ[f + m] for m in range(many)]))
        for m in range(many):
            y = r[:, m * elems : (m + 1) * elems]
            parts[turn, f + m] = y[:rows]
            y = y[rows:]
            for j in range(nj):
                own[j, f + m] = y[j * fp : (j + 1) * fp]

    lists = [roll(rim[...], elems // 2)] + [code[j : j + 1, :] for j in range(1, nj)]
    maps, hots = [], []
    for row in lists:
        group = jnp.zeros_like(row)
        for k in range(1, nk):
            group = group + jnp.where(row >= k * elems, 1, 0)
        maps.append(group)
        hit = lax.broadcasted_iota(jnp.int32, (elems, elems), 0) == row - group * elems
        hots.append(jnp.where(hit, 1.0, 0.0).astype(F32))
    column = jnp.concatenate(hots, axis=1).astype(BF16)
    whole = jnp.concatenate([integ[f] for f in range(nf)], axis=0)
    high, low = halves(whole)
    tall = up(nf * cp, 16)
    gathered[...] = mul(
        jnp.concatenate([stacked([high], tall), stacked([low], tall)], axis=1),
        jnp.concatenate([column, column], axis=0),
    )

    def near_traces(i, store):
        which = jnp.broadcast_to(maps[i], (fp, elems))
        for f in range(0, nf, many):
            at = slice(i * elems, (i + 1) * elems)
            r = mul(
                a_near,
                spread_out([gathered[(f + m) * cp : (f + m + 1) * cp, at] for m in range(many)]),
            )
            for m in range(many):
                y = r[:, m * elems : (m + 1) * elems]
                total = y[:fp]
                for k in range(1, nk):
                    total = jnp.where(which == k, y[k * fp : (k + 1) * fp], total)
                store(f + m, total)

    e_lane = lax.broadcasted_iota(jnp.int32, (1, elems), 1)
    lower = e_lane < elems // 2
    fh = fp // 2

    def store_rim(f, total):
        top, turned = total[:fh], roll(total[fh:], elems // 2)
        rim_send[0, f] = jnp.where(lower, top, turned)
        rim_send[1, f] = jnp.where(lower, turned, top)

    near_traces(0, store_rim)

    @pl.when(jnp.logical_not(corner))
    def _():
        begin_rim()

    for j in range(1, nj):

        def store_near(f, total, j=j):
            near[j - 1, f] = total

        near_traces(j, store_near)

    for f in range(0, nf, many):
        group = mixed(turn, range(f, f + many))
        for m in range(many):
            base[f + m] = group[m]

    @pl.when(corner)
    def _():
        pl.semaphore_wait(barrier, greeted)
        begin(par_copies + fric_copies)
        begin_rim()

    arrive(5, 6, 7)
    for j in range(nj):
        for q in range(nfm):
            w_lift[j * fp + q : j * fp + q + 1, :nb] = face_lift[q, pl.ds(j, 1), :]
    def face_flux(j, at_row, field):
        def step(i, carry):
            f = i * many
            sums = [None] * many
            for g in range(nf):
                mine, other = own[j, g], field(g)
                for m in range(many):
                    term = own_flux[f + m, g, pl.ds(j, 1), :] * mine
                    term = term + neighbour_flux[f + m, g, pl.ds(j, 1), :] * other
                    sums[m] = term if sums[m] is None else sums[m] + term
            for m in range(many):
                at = pl.ds(pl.multiple_of((f + m) * elems, elems), elems)
                flux[at_row : at_row + fp, at] = sums[m]
            return carry

        lax.fori_loop(0, nf // many, step, 0)

    kj = (nj - 1) * fp
    kr = up(kj, 16)
    for j in range(1, nj):
        face_flux(j, (j - 1) * fp, lambda g, j=j: near[j - 1, g])
    lift_all = w_lift[...].T[:cp]
    lift = roll(lift_all, 128 - fp)
    l_hi, l_lo = halves(lift)
    l_hi, l_lo = l_hi[:, :kr], l_lo[:, :kr]
    k_lane = lax.broadcasted_iota(jnp.int32, lift_all.shape, 1)
    x = flux[:kj]
    high, low = halves(x)
    x_hi = stacked([high], kr)
    r = mul(stacked([l_hi, l_lo], 2 * cp), x_hi)
    r = r[:cp] + r[cp:] + mul(l_hi.astype(BF16), stacked([low], kr))
    for f in range(nf):
        base[f] = base[f] - r[:, f * elems : (f + 1) * elems]

    for copy in par_copies:
        copy.wait_recv()
    state = par_recv[:, 0].reshape(slots, 128)
    slip = friction(normal_here, locked_here, state, par_recv[:, 1].reshape(slots, 128))
    signed = jnp.where(locked_here < 0.0, -slip, jnp.where(locked_here > 0.0, slip, 0.0))
    point = lax.broadcasted_iota(jnp.int32, (1, 128), 1)
    signed = jnp.where(point < nq, signed, 0.0)

    arrive(12, 14, 15, 18)
    for k in range(nface):
        for b in range(nb):
            w_flift[k * cp + b : k * cp + b + 1, :nq] = fault_lift[b, pl.ds(k, 1), :]
    live = jnp.zeros_like(lane)
    for o in range(n_group):
        live = jnp.where(slot_group == o, send_count[0, o], live)
    live = (lane & (CAP - 1)) < live
    side = jnp.where(live, face_row, -1)
    hot0 = jnp.where(is_v1, 0.0, hot)
    hot1 = jnp.where(is_v1, hot, 0.0)
    spread = stacked([hot0, hot1], 2 * elems)
    f_hi, f_lo = halves(w_flift[...])
    kq = 64
    a_lift = jnp.concatenate([f_hi + roll(f_lo, kq), f_hi], axis=1)[:, : 3 * kq].astype(BF16)
    turned = roll(mean, slots)
    locked = jnp.where(is_v1, mean, turned)
    drive_0 = jnp.where(is_v1, 0.5 * (roll(sides, 2 * slots) - sides), locked - sides)
    drive_1 = jnp.where(is_v1, 0.5 * sign_i, -1.0)
    answer = jnp.concatenate([signed] * 4, axis=0).T[:qp]
    drive = drive_0 + drive_1 * answer
    high, low = halves(drive)
    gap = jnp.zeros((kq - qp, width), F32)
    y = mul(a_lift, stacked([high, gap, high, gap, low, gap], 3 * kq))
    lifted = jnp.where(side == 0, y[:cp], 0.0)
    for k in range(1, nface):
        lifted = jnp.where(side == k, y[k * cp : (k + 1) * cp], lifted)
    high, low = halves(lifted)
    z = lax.dot_general(
        stacked([high, low], 2 * cp),
        spread,
        (((1,), (1,)), ((), ())),
        preferred_element_type=F32,
    )
    z = z[:cp] + z[cp:]
    by_traction, by_jump = z[:, :elems], z[:, elems:]
    for copy, there in zip(rim_copies, (has_prev, has_next)):
        pl.when(there)(copy.wait_recv)
    from_prev = lower & has_prev
    from_next = jnp.logical_not(lower) & has_next
    for f in range(nf):
        x, y = rim_recv[0, f], rim_recv[1, f]
        for i, (x, y) in enumerate(((x, y), (roll(x, elems // 2), roll(y, elems // 2)))):
            near[0, f, i * fh : (i + 1) * fh] = jnp.where(from_prev, x, jnp.where(from_next, y, 0.0))
    face_flux(0, 0, lambda g: near[0, g])
    high, low = halves(flux[:fp])
    l0 = lanes3(jnp.where(k_lane < fp, lift_all, 0.0), fp)[:, : 3 * fp]
    r = mul(l0, stacked([high, high, low], 3 * fp))

    for f in range(nf):
        add = coupling[0, f] * by_traction + coupling[1, f] * by_jump
        total = base[f] - r[:, f * elems : (f + 1) * elems] + add
        out[f] = dofs[f] + total[:nb]


    for copy in fric_copies:
        copy.wait_recv()
    state = par[0]
    slip = friction(
        fric_recv[:, 0].reshape(slots, 128)[:, :nq],
        fric_recv[:, 1].reshape(slots, 128)[:, :nq],
        state,
        par[1],
    )
    out_state[...] = state + 0.5 * evolution_rate[...] * (jnp.exp(-state) - slip)

    for copy in par_copies + fric_copies:
        copy.wait_send()
    for copy, there in zip(rim_copies, (has_next, has_prev)):
        pl.when(there)(copy.wait_send)


def finish(dofs, state, out, out_state, sem):
    copies = [
        pltpu.make_async_copy(dofs, out, sem.at[0]),
        pltpu.make_async_copy(state, out_state, sem.at[1]),
    ]
    for copy in copies:
        copy.start()
    for copy in copies:
        copy.wait()


def body(*args):
    args = list(args)
    n_group, n_sub = lax.axis_size("group"), lax.axis_size("sub")
    orders = {1: (1, 2, 0, 3), 3: (1, 0, 2), 5: (1, 2, 0, 3), 6: (1, 2, 0, 3), 7: (2, 0, 1)}
    orders |= {13: (2, 0, 1), 14: (1, 0, 2)}
    orders |= {i: (1, 0) for i in (12, 15, 16, 17, 18)}
    for i, order in orders.items():
        args[i] = jnp.transpose(args[i], order)
    nf, nb, elems = args[0].shape
    nfm, nj, _ = args[3].shape
    nk = args[4].shape[0]
    ndim = args[2].shape[0]
    _, nface, nq = args[13].shape
    slots = args[10].shape[1]
    args[9] = args[9].reshape(1, elems)
    cp, fp, qp = up(nb, 8), up(nfm, 8), up(nq, 8)
    width = 4 * slots
    vmem = pl.BlockSpec(memory_space=pltpu.VMEM)
    anywhere = pl.BlockSpec(memory_space=pl.ANY)
    held = [(pltpu.SMEM if i in (12, 15) else pltpu.VMEM)(a.shape, a.dtype) for i, a in enumerate(args)]
    shapes = (args[0].shape, args[16].shape)
    copies = 2 * (n_group - 1) + 2
    dofs, state = pl.pallas_call(
        functools.partial(kernel, n_group, n_sub),
        out_shape=tuple(pltpu.VMEM(s, F32) for s in shapes),
        in_specs=[anywhere] * len(args),
        out_specs=(vmem, vmem),
        scratch_shapes=held[:16]
        + held[18:]
        + [
            pltpu.VMEM((2,) + args[16].shape, F32),
            pltpu.VMEM((nf, cp, elems), F32),
            pltpu.VMEM((2, nf, ndim * cp, elems), F32),
            pltpu.VMEM((up(nf * cp, 16), nj * elems), F32),
            pltpu.VMEM((nj, nf, fp, elems), F32),
            pltpu.VMEM((nj, nf, fp, elems), F32),
            pltpu.VMEM((up((nj - 1) * fp, 16), nf * elems), F32),
            pltpu.VMEM((nf, cp, elems), F32),
            pltpu.VMEM((ndim * cp, 128), F32),
            pltpu.VMEM((nj * fp, 128), F32),
            pltpu.VMEM((nk * fp, 128), F32),
            pltpu.VMEM((nface, cp, 128), F32),
            pltpu.VMEM((nface * cp, 128), F32),
            pltpu.VMEM((128, 128), F32),
            pltpu.VMEM((2, nf, fp // 2, elems), F32),
            pltpu.VMEM((2, nf, fp // 2, elems), F32),
        ]
        + [pltpu.VMEM((n_group, 2, CAP, 128), F32)] * 4
        + [
            pltpu.SemaphoreType.DMA((len(TOGETHER),)),
            pltpu.SemaphoreType.DMA((copies,)),
            pltpu.SemaphoreType.DMA((copies,)),
        ],
        compiler_params=pltpu.CompilerParams(collective_id=0, has_side_effects=True),
    )(*args)
    dofs, state = pl.pallas_call(
        finish,
        out_shape=tuple(jax.ShapeDtypeStruct(s, F32) for s in shapes),
        in_specs=[vmem, vmem],
        out_specs=(anywhere, anywhere),
        scratch_shapes=[pltpu.SemaphoreType.DMA((2,))],
        compiler_params=pltpu.CompilerParams(vmem_limit_bytes=8 << 20),
    )(dofs, state)
    return dofs, state.T


def solution(mesh):
    both = ("group", "sub")
    placed = (
        P(None, None, both),
        P(None, None, None, both),
        P(),
        P(),
        P(),
        P(None, None, None, both),
        P(None, None, None, both),
        P(),
        P(None, both),
        P(both),
        P(None, both),
        P(None, both),
        P(None, both),
        P(),
        P(),
        P(),
        P(None, both),
        P(None, both),
        P(None, both),
    )
    return jax.shard_map(
        body,
        mesh=mesh,
        in_specs=placed,
        out_specs=(P(None, None, both), P(None, both)),
        check_vma=False,
    )
```

```python
import functools

import jax
import jax.numpy as jnp
from jax import lax
from jax.experimental import pallas as pl
from jax.experimental.pallas import tpu as pltpu
from jax.sharding import PartitionSpec as P

DERIV = 4
NEWTON = 3
CAP = 8
F32 = jnp.float32
BF16 = jnp.bfloat16
MESH = pl.DeviceIdType.MESH


def up(n, m):
    return (n + m - 1) // m * m


def halves(x):
    high = x.astype(BF16).astype(F32)
    return high, x - high


def stacked(parts, rows):
    have = sum(p.shape[0] for p in parts)
    if have < rows:
        parts = parts + [jnp.zeros((rows - have, parts[0].shape[1]), F32)]
    return jnp.concatenate(parts, axis=0).astype(BF16)


def mul(a, b):
    return lax.dot_general(a, b, (((1,), (0,)), ((), ())), preferred_element_type=F32)


def roll(x, shift):
    return pltpu.roll(x, shift, 1)


def lanes3(a, step):
    high, low = halves(a)
    return (high + roll(low, step) + roll(high, 2 * step)).astype(BF16)


def friction(normal, locked, state, direct):
    rate = 0.5 * jnp.exp(state / direct)
    x = 2.0 - normal
    load = jnp.maximum(x, 0.0) + jnp.log1p(jnp.exp(-jnp.abs(x)))
    strength = load * direct
    magnitude = jnp.abs(locked)
    slip = magnitude / (1.0 + strength * rate)
    for _ in range(1, NEWTON):
        scaled = rate * slip
        root = jnp.sqrt(1.0 + scaled * scaled)
        log = jnp.log(jnp.abs(scaled) + root)
        log = jnp.where(scaled < 0.0, -log, log)
        slip = slip - (slip + strength * log - magnitude) / (1.0 + strength * rate / root)
    return slip


N_IN = 19
ORDER = (2, 0, 1, 13, 10, 11, 16, 17, 4, 3, 9, 8, 7, 14, 18, 12, 15, 5, 6)

TOGETHER = ((2,), (0,), (1,), (10, 11, 13, 16, 17), (3, 4, 8, 9), (5, 6, 7), (12, 14, 15, 18))
SEM = {i: n for n, members in enumerate(TOGETHER) for i in members}


def kernel(n_group, n_sub, *refs):
    hbm, out, out_state = refs[:N_IN], refs[N_IN], refs[N_IN + 1]
    local = refs[N_IN + 2 : 2 * N_IN]
    (
        par,
        integ,
        parts,
        gathered,
        own,
        near,
        flux,
        base,
        w_stiff,
        w_face,
        w_near,
        w_ftrace,
        w_flift,
        w_lift,
        rim_send,
        rim_recv,
        fric_send,
        fric_recv,
        par_send,
        par_recv,
        stage_sem,
        send_sem,
        recv_sem,
    ) = refs[2 * N_IN :]
    me_g = lax.axis_index("group")
    me_s = lax.axis_index("sub")
    has_prev = me_s > 0
    has_next = me_s < n_sub - 1
    barrier = pltpu.get_barrier_semaphore()
    for d in range(1, n_group):
        pl.semaphore_signal(
            barrier, inc=1, device_id=(lax.rem(me_g + d, n_group), me_s), device_id_type=MESH
        )
    for side, s in ((has_prev, me_s - 1), (has_next, me_s + 1)):

        @pl.when(side)
        def _(s=s):
            pl.semaphore_signal(barrier, inc=1, device_id=(me_g, s), device_id_type=MESH)

    greeted = n_group - 1 + jnp.where(has_prev, 1, 0) + jnp.where(has_next, 1, 0)

    held = list(local[:16]) + [par.at[0], par.at[1]] + list(local[16:])
    staged = {i: pltpu.make_async_copy(hbm[i], held[i], stage_sem.at[SEM[i]]) for i in ORDER}
    for i in ORDER:
        staged[i].start()

    def arrive(*which):
        for i in which:
            staged[i].wait()

    (
        dofs,
        jac,
        stiff,
        face_trace,
        neighbour_trace,
        own_flux,
        neighbour_flux,
        face_lift,
        code,
        rim,
        fault_element,
        fault_face,
        send_count,
        fault_trace,
        fault_lift,
        coupling,
    ) = held[:16]
    evolution_rate = held[18]
    nf, nb, elems = dofs.shape
    ndim = stiff.shape[0]
    nfm, nj, _ = face_trace.shape
    nk = neighbour_trace.shape[0]
    _, nface, nq = fault_trace.shape
    slots = fault_element.shape[1]
    cp, fp, qp = up(nb, 8), up(nfm, 8), up(nq, 8)
    width = 4 * slots

    w_stiff[...] = jnp.zeros_like(w_stiff)
    w_ftrace[...] = jnp.zeros_like(w_ftrace)
    w_face[...] = jnp.zeros_like(w_face)
    w_near[...] = jnp.zeros_like(w_near)
    w_flift[...] = jnp.zeros_like(w_flift)
    w_lift[...] = jnp.zeros_like(w_lift)
    par_send[...] = jnp.ones_like(par_send)

    def to_group(src, dst, first):
        copies = []
        for d in range(1, n_group):
            o = lax.rem(me_g + d, n_group)
            copies.append(
                pltpu.make_async_remote_copy(
                    src_ref=src.at[o],
                    dst_ref=dst.at[me_g],
                    send_sem=send_sem.at[first + d - 1],
                    recv_sem=recv_sem.at[first + d - 1],
                    device_id=(o, me_s),
                    device_id_type=MESH,
                )
            )
        return copies

    par_copies = to_group(par_send, par_recv, 0)
    fric_copies = to_group(fric_send, fric_recv, n_group - 1)
    rim_copies = []
    for side, s in enumerate((me_s + 1, me_s - 1)):
        rim_copies.append(
            pltpu.make_async_remote_copy(
                src_ref=rim_send.at[side],
                dst_ref=rim_recv.at[side],
                send_sem=send_sem.at[2 * (n_group - 1) + side],
                recv_sem=recv_sem.at[2 * (n_group - 1) + side],
                device_id=(me_g, s),
                device_id_type=MESH,
            )
        )

    def begin(copies):
        for copy in copies:
            copy.start()

    def begin_rim():
        for copy, there in zip(rim_copies, (has_next, has_prev)):
            pl.when(there)(copy.start)

    first_row = me_g == 0
    far = me_g >= max(n_group // 2, 1)
    middle = jnp.logical_not(first_row | far)
    corner = first_row & (me_s == 0)

    arrive(2)
    for d in range(ndim):
        w_stiff[d * cp : d * cp + nb, :nb] = stiff[d]
    a_stiff = lanes3(-w_stiff[...], cp)
    many = 3 if nf % 3 == 0 else 1
    rows = ndim * cp

    def spread_out(fields):
        out = []
        for x in fields:
            high, low = halves(x)
            out.append(stacked([high, high, low], 128))
        return jnp.concatenate(out, axis=1)

    def mixed(turn, fields):
        sums = [None] * len(fields)
        for g in range(nf):
            for d in range(ndim):
                x = parts[turn, g, d * cp : (d + 1) * cp]
                for m, f in enumerate(fields):
                    term = jac[f, g, pl.ds(d, 1), :] * x
                    sums[m] = term if sums[m] is None else sums[m] + term
        return sums

    arrive(0)
    for f in range(0, nf, many):
        group = [
            jnp.concatenate([dofs[f + m], jnp.zeros((cp - nb, elems), F32)], axis=0)
            for m in range(many)
        ]
        r = mul(a_stiff, spread_out(group))
        for m in range(many):
            integ[f + m] = group[m]
            parts[0, f + m] = r[:, m * elems : (m + 1) * elems]

    arrive(1)
    arrive(10, 11, 13, 16, 17)
    for o in range(n_group):
        for i in range(2):
            par_send[o, i, :, :nq] = par[i, o * CAP : (o + 1) * CAP, :]
    par_recv[me_g] = par_send[me_g]

    for k in range(nface):
        for b in range(nb):
            w_ftrace[k, b : b + 1, :nq] = fault_trace[b, pl.ds(k, 1), :]
    lane = lax.broadcasted_iota(jnp.int32, (1, width), 1)
    is_v1 = (lane & slots) != 0
    sign_i = jnp.where((lane & (2 * slots)) != 0, 1.0, -1.0).astype(F32)
    slot_group = (lane & (slots - 1)) // CAP
    elem = fault_element[...]
    face = fault_face[...]
    elem_row = jnp.concatenate([elem[0:1], elem[0:1], elem[1:2], elem[1:2]], axis=1)
    face_row = jnp.concatenate([face[0:1], face[0:1], face[1:2], face[1:2]], axis=1)
    hit = lax.broadcasted_iota(jnp.int32, (elems, width), 0) == elem_row
    hot = jnp.where(hit, 1.0, 0.0).astype(F32)

    a_fault = []
    for k in range(nface):
        high, low = halves(w_ftrace[k])
        gap = jnp.zeros((128 - 3 * cp, 128), F32)
        a_fault.append(jnp.concatenate([high, low, high, gap], axis=0).T[:qp])
    a_fault = jnp.concatenate(a_fault, axis=0).astype(BF16)

    half_hot = 0.5 * hot
    weights = (
        jnp.where(is_v1, 0.0, half_hot),
        jnp.where(is_v1, half_hot, 0.0),
        jnp.where(is_v1, sign_i * half_hot, 0.0),
    )
    mixing = jnp.concatenate([w for w in weights for _ in range(2)], axis=0).astype(BF16)
    hot_16 = hot.astype(BF16)
    factorial = 1.0
    for degree in range(1, DERIV):
        factorial = factorial * (degree + 1)
        turn = (degree - 1) % 2
        for f in range(0, nf, many):
            group = mixed(turn, range(f, f + many))
            for m in range(many):
                integ[f + m] = integ[f + m] + group[m] / factorial
            r = mul(a_stiff, spread_out(group))
            for m in range(many):
                parts[1 - turn, f + m] = r[:, m * elems : (m + 1) * elems]
        if degree == 1:

            @pl.when(far)
            def _():
                pl.semaphore_wait(barrier, greeted)
                begin(par_copies)

        if degree == 2:
            @pl.when(middle)
            def _():
                pl.semaphore_wait(barrier, greeted)
                begin(par_copies)

    factorial = factorial * (DERIV + 1)

    def finished(fields):
        for f, x in zip(fields, mixed((DERIV - 1) % 2, fields)):
            integ[f] = integ[f] + x / factorial

    picked = (0, 3, 7)
    finished(picked)

    def fault_sides(x):
        high, low = halves(x)
        y = mul(a_fault, stacked([high, high, low], 128))
        total = jnp.where(face_row == 0, y[:qp], 0.0)
        for k in range(1, nface):
            total = jnp.where(face_row == k, y[k * qp : (k + 1) * qp], total)
        return total

    tall = up(cp, 16)
    split = [stacked([p], tall) for f in picked for p in halves(integ[f])]
    mean = fault_sides(mul(jnp.concatenate(split, axis=1), mixing)[:cp])
    mean_t = jnp.concatenate([mean, jnp.zeros((128 - qp, width), F32)], axis=0).T
    mean_t = mean_t[: 2 * slots] + mean_t[2 * slots :]
    normal_here = mean_t[:slots]
    locked_here = mean_t[slots:]
    for o in range(n_group):
        fric_send[o, 0] = normal_here[o * CAP : (o + 1) * CAP]
        fric_send[o, 1] = locked_here[o * CAP : (o + 1) * CAP]
    fric_recv[me_g] = fric_send[me_g]

    @pl.when(jnp.logical_not(first_row))
    def _():
        begin(fric_copies)

    @pl.when(first_row & (me_s > 0))
    def _():
        pl.semaphore_wait(barrier, greeted)
        begin(par_copies + fric_copies)

    rest = [f for f in range(nf) if f not in picked]
    for i in range(0, len(rest), many):
        finished(rest[i : i + many])

    arrive(3, 4, 8, 9)
    for k in range(nk):
        w_near[k * fp : k * fp + nfm, :nb] = neighbour_trace[k]
    a_near = lanes3(w_near[...], cp)
    lists = [roll(rim[...], elems // 2)] + [code[j : j + 1, :] for j in range(1, nj)]
    maps, hots = [], []
    for row in lists:
        group = jnp.zeros_like(row)
        for k in range(1, nk):
            group = group + jnp.where(row >= k * elems, 1, 0)
        maps.append(group)
        hit = lax.broadcasted_iota(jnp.int32, (elems, elems), 0) == row - group * elems
        hots.append(jnp.where(hit, 1.0, 0.0).astype(F32))
    column = jnp.concatenate(hots, axis=1).astype(BF16)
    whole = jnp.concatenate([integ[f] for f in range(nf)], axis=0)
    high, low = halves(whole)
    tall = up(nf * cp, 16)
    gathered[...] = mul(
        jnp.concatenate([stacked([high], tall), stacked([low], tall)], axis=1),
        jnp.concatenate([column, column], axis=0),
    )

    def near_traces(i, store):
        which = jnp.broadcast_to(maps[i], (fp, elems))
        for f in range(0, nf, many):
            at = slice(i * elems, (i + 1) * elems)
            r = mul(
                a_near,
                spread_out([gathered[(f + m) * cp : (f + m + 1) * cp, at] for m in range(many)]),
            )
            for m in range(many):
                y = r[:, m * elems : (m + 1) * elems]
                total = y[:fp]
                for k in range(1, nk):
                    total = jnp.where(which == k, y[k * fp : (k + 1) * fp], total)
                store(f + m, total)

    e_lane = lax.broadcasted_iota(jnp.int32, (1, elems), 1)
    lower = e_lane < elems // 2
    fh = fp // 2

    def store_rim(f, total):
        top, turned = total[:fh], roll(total[fh:], elems // 2)
        rim_send[0, f] = jnp.where(lower, top, turned)
        rim_send[1, f] = jnp.where(lower, turned, top)

    near_traces(0, store_rim)

    @pl.when(jnp.logical_not(corner))
    def _():
        begin_rim()

    highs, lows = zip(*[halves(integ[f]) for f in picked[1:]])
    g = mul(stacked(list(highs) + list(lows), 4 * cp), hot_16)
    g = g[: 2 * cp] + g[2 * cp :]
    sides = fault_sides(jnp.where(is_v1, g[cp:], g[:cp]))
    for j in range(nj):
        for q in range(nfm):
            w_face[j * fp + q : j * fp + q + 1, :nb] = face_trace[q, pl.ds(j, 1), :]
    gap = jnp.zeros((128 - cp, 128), F32)
    v = [jnp.concatenate([w_stiff[d * cp : (d + 1) * cp], gap], axis=0).T[:cp] for d in range(ndim)]
    a_last = jnp.concatenate(
        [lanes3(jnp.concatenate(v, axis=0), cp), lanes3(w_face[...], cp)], axis=0
    )
    turn = DERIV % 2
    for f in range(0, nf, many):
        r = mul(a_last, spread_out([integ[f + m] for m in range(many)]))
        for m in range(many):
            y = r[:, m * elems : (m + 1) * elems]
            parts[turn, f + m] = y[:rows]
            y = y[rows:]
            for j in range(nj):
                own[j, f + m] = y[j * fp : (j + 1) * fp]

    for j in range(1, nj):

        def store_near(f, total, j=j):
            near[j - 1, f] = total

        near_traces(j, store_near)

    for f in range(0, nf, many):
        group = mixed(turn, range(f, f + many))
        for m in range(many):
            base[f + m] = group[m]

    @pl.when(corner)
    def _():
        pl.semaphore_wait(barrier, greeted)
        begin(par_copies + fric_copies)
        begin_rim()

    arrive(5, 6, 7)
    for j in range(nj):
        for q in range(nfm):
            w_lift[j * fp + q : j * fp + q + 1, :nb] = face_lift[q, pl.ds(j, 1), :]
    def face_flux(j, at_row, field):
        def step(i, carry):
            f = i * many
            sums = [None] * many
            for g in range(nf):
                mine, other = own[j, g], field(g)
                for m in range(many):
                    term = own_flux[f + m, g, pl.ds(j, 1), :] * mine
                    term = term + neighbour_flux[f + m, g, pl.ds(j, 1), :] * other
                    sums[m] = term if sums[m] is None else sums[m] + term
            for m in range(many):
                at = pl.ds(pl.multiple_of((f + m) * elems, elems), elems)
                flux[at_row : at_row + fp, at] = sums[m]
            return carry

        lax.fori_loop(0, nf // many, step, 0)

    kj = (nj - 1) * fp
    kr = up(kj, 16)
    for j in range(1, nj):
        face_flux(j, (j - 1) * fp, lambda g, j=j: near[j - 1, g])
    lift_all = w_lift[...].T[:cp]
    lift = roll(lift_all, 128 - fp)
    l_hi, l_lo = halves(lift)
    l_hi, l_lo = l_hi[:, :kr], l_lo[:, :kr]
    k_lane = lax.broadcasted_iota(jnp.int32, lift_all.shape, 1)
    x = flux[:kj]
    high, low = halves(x)
    x_hi = stacked([high], kr)
    r = mul(stacked([l_hi, l_lo], 2 * cp), x_hi)
    r = r[:cp] + r[cp:] + mul(l_hi.astype(BF16), stacked([low], kr))
    for f in range(nf):
        base[f] = base[f] - r[:, f * elems : (f + 1) * elems]

    for copy in par_copies:
        copy.wait_recv()
    state = par_recv[:, 0].reshape(slots, 128)
    slip = friction(normal_here, locked_here, state, par_recv[:, 1].reshape(slots, 128))
    signed = jnp.where(locked_here < 0.0, -slip, jnp.where(locked_here > 0.0, slip, 0.0))
    point = lax.broadcasted_iota(jnp.int32, (1, 128), 1)
    signed = jnp.where(point < nq, signed, 0.0)

    arrive(12, 14, 15, 18)
    for k in range(nface):
        for b in range(nb):
            w_flift[k * cp + b : k * cp + b + 1, :nq] = fault_lift[b, pl.ds(k, 1), :]
    live = jnp.zeros_like(lane)
    for o in range(n_group):
        live = jnp.where(slot_group == o, send_count[0, o], live)
    live = (lane & (CAP - 1)) < live
    side = jnp.where(live, face_row, -1)
    hot0 = jnp.where(is_v1, 0.0, hot)
    hot1 = jnp.where(is_v1, hot, 0.0)
    spread = stacked([hot0, hot1], 2 * elems)
    f_hi, f_lo = halves(w_flift[...])
    kq = 64
    a_lift = jnp.concatenate([f_hi + roll(f_lo, kq), f_hi], axis=1)[:, : 3 * kq].astype(BF16)
    mean = mean + roll(mean, 2 * slots)
    turned = roll(mean, slots)
    locked = jnp.where(is_v1, mean, turned)
    drive_0 = jnp.where(is_v1, 0.5 * (roll(sides, 2 * slots) - sides), locked - sides)
    drive_1 = jnp.where(is_v1, 0.5 * sign_i, -1.0)
    answer = jnp.concatenate([signed] * 4, axis=0).T[:qp]
    drive = drive_0 + drive_1 * answer
    high, low = halves(drive)
    gap = jnp.zeros((kq - qp, width), F32)
    y = mul(a_lift, stacked([high, gap, high, gap, low, gap], 3 * kq))
    lifted = jnp.where(side == 0, y[:cp], 0.0)
    for k in range(1, nface):
        lifted = jnp.where(side == k, y[k * cp : (k + 1) * cp], lifted)
    high, low = halves(lifted)
    z = lax.dot_general(
        stacked([high, low], 2 * cp),
        spread,
        (((1,), (1,)), ((), ())),
        preferred_element_type=F32,
    )
    z = z[:cp] + z[cp:]
    by_traction, by_jump = z[:, :elems], z[:, elems:]
    for copy, there in zip(rim_copies, (has_prev, has_next)):
        pl.when(there)(copy.wait_recv)
    from_prev = lower & has_prev
    from_next = jnp.logical_not(lower) & has_next
    for f in range(nf):
        x, y = rim_recv[0, f], rim_recv[1, f]
        for i, (x, y) in enumerate(((x, y), (roll(x, elems // 2), roll(y, elems // 2)))):
            near[0, f, i * fh : (i + 1) * fh] = jnp.where(from_prev, x, jnp.where(from_next, y, 0.0))
    face_flux(0, 0, lambda g: near[0, g])
    high, low = halves(flux[:fp])
    l0 = lanes3(jnp.where(k_lane < fp, lift_all, 0.0), fp)[:, : 3 * fp]
    r = mul(l0, stacked([high, high, low], 3 * fp))

    for f in range(nf):
        add = coupling[0, f] * by_traction + coupling[1, f] * by_jump
        total = base[f] - r[:, f * elems : (f + 1) * elems] + add
        out[f] = dofs[f] + total[:nb]


    for copy in fric_copies:
        copy.wait_recv()
    state = par[0]
    slip = friction(
        fric_recv[:, 0].reshape(slots, 128)[:, :nq],
        fric_recv[:, 1].reshape(slots, 128)[:, :nq],
        state,
        par[1],
    )
    out_state[...] = state + 0.5 * evolution_rate[...] * (jnp.exp(-state) - slip)

    for copy in par_copies + fric_copies:
        copy.wait_send()
    for copy, there in zip(rim_copies, (has_next, has_prev)):
        pl.when(there)(copy.wait_send)


def finish(dofs, state, out, out_state, sem):
    copies = [
        pltpu.make_async_copy(dofs, out, sem.at[0]),
        pltpu.make_async_copy(state, out_state, sem.at[1]),
    ]
    for copy in copies:
        copy.start()
    for copy in copies:
        copy.wait()


def body(*args):
    args = list(args)
    n_group, n_sub = lax.axis_size("group"), lax.axis_size("sub")
    orders = {1: (1, 2, 0, 3), 3: (1, 0, 2), 5: (1, 2, 0, 3), 6: (1, 2, 0, 3), 7: (2, 0, 1)}
    orders |= {13: (2, 0, 1), 14: (1, 0, 2)}
    orders |= {i: (1, 0) for i in (12, 15, 16, 17, 18)}
    for i, order in orders.items():
        args[i] = jnp.transpose(args[i], order)
    nf, nb, elems = args[0].shape
    nfm, nj, _ = args[3].shape
    nk = args[4].shape[0]
    ndim = args[2].shape[0]
    _, nface, nq = args[13].shape
    slots = args[10].shape[1]
    args[9] = args[9].reshape(1, elems)
    cp, fp, qp = up(nb, 8), up(nfm, 8), up(nq, 8)
    width = 4 * slots
    vmem = pl.BlockSpec(memory_space=pltpu.VMEM)
    anywhere = pl.BlockSpec(memory_space=pl.ANY)
    held = [(pltpu.SMEM if i in (12, 15) else pltpu.VMEM)(a.shape, a.dtype) for i, a in enumerate(args)]
    shapes = (args[0].shape, args[16].shape)
    copies = 2 * (n_group - 1) + 2
    dofs, state = pl.pallas_call(
        functools.partial(kernel, n_group, n_sub),
        out_shape=tuple(pltpu.VMEM(s, F32) for s in shapes),
        in_specs=[anywhere] * len(args),
        out_specs=(vmem, vmem),
        scratch_shapes=held[:16]
        + held[18:]
        + [
            pltpu.VMEM((2,) + args[16].shape, F32),
            pltpu.VMEM((nf, cp, elems), F32),
            pltpu.VMEM((2, nf, ndim * cp, elems), F32),
            pltpu.VMEM((up(nf * cp, 16), nj * elems), F32),
            pltpu.VMEM((nj, nf, fp, elems), F32),
            pltpu.VMEM((nj, nf, fp, elems), F32),
            pltpu.VMEM((up((nj - 1) * fp, 16), nf * elems), F32),
            pltpu.VMEM((nf, cp, elems), F32),
            pltpu.VMEM((ndim * cp, 128), F32),
            pltpu.VMEM((nj * fp, 128), F32),
            pltpu.VMEM((nk * fp, 128), F32),
            pltpu.VMEM((nface, cp, 128), F32),
            pltpu.VMEM((nface * cp, 128), F32),
            pltpu.VMEM((128, 128), F32),
            pltpu.VMEM((2, nf, fp // 2, elems), F32),
            pltpu.VMEM((2, nf, fp // 2, elems), F32),
        ]
        + [pltpu.VMEM((n_group, 2, CAP, 128), F32)] * 4
        + [
            pltpu.SemaphoreType.DMA((len(TOGETHER),)),
            pltpu.SemaphoreType.DMA((copies,)),
            pltpu.SemaphoreType.DMA((copies,)),
        ],
        compiler_params=pltpu.CompilerParams(collective_id=0, has_side_effects=True),
    )(*args)
    dofs, state = pl.pallas_call(
        finish,
        out_shape=tuple(jax.ShapeDtypeStruct(s, F32) for s in shapes),
        in_specs=[vmem, vmem],
        out_specs=(anywhere, anywhere),
        scratch_shapes=[pltpu.SemaphoreType.DMA((2,))],
        compiler_params=pltpu.CompilerParams(vmem_limit_bytes=8 << 20),
    )(dofs, state)
    return dofs, state.T


def solution(mesh):
    both = ("group", "sub")
    placed = (
        P(None, None, both),
        P(None, None, None, both),
        P(),
        P(),
        P(),
        P(None, None, None, both),
        P(None, None, None, both),
        P(),
        P(None, both),
        P(both),
        P(None, both),
        P(None, both),
        P(None, both),
        P(),
        P(),
        P(),
        P(None, both),
        P(None, both),
        P(None, both),
    )
    return jax.shard_map(
        body,
        mesh=mesh,
        in_specs=placed,
        out_specs=(P(None, None, both), P(None, both)),
        check_vma=False,
    )
```
